32 devices in a mesh: seq: 8 (over z, x), tp: 4 (over y, core).
Axes of the slice: x: 2, y: 2, z: 4, core: 2. Of those that a mesh axis runs over, the one named last changes fastest.
Arguments:
- draft_q: bfloat16 [256, 4096], P('seq', 'tp'), may hold values from -48 to 48
- draft_k: bfloat16 [256, 1024], P('seq', 'tp'), may hold values from -24 to 24
- draft_v: bfloat16 [256, 1024], P('seq', 'tp'), may hold values from -6 to 6
- cache_k: bfloat16 [4, 8192, 1024], P(None, 'seq', 'tp'), may hold values from -6 to 6
- cache_v: bfloat16 [4, 8192, 1024], P(None, 'seq', 'tp'), may hold values from -6 to 6
- lengths: int32 [4], replicated, may hold values from 2 to 8184, as said below
- migrating: int32 [4], replicated, may hold values from 0 to 1, as said below
- parents: int32 [4, 64], replicated, may hold values from -1 to 62, as said below
- accepted: int32 [4, 8], replicated, may hold values from -1 to 63, as said below
- out_weight: bfloat16 [4096, 4096], P('tp'), may hold values from -0.09375 to 0.09375
Outputs:
- attn_out: bfloat16 [256, 4096], P('seq', 'tp')
- new_k: bfloat16 [4, 8192, 1024], P(None, 'seq', 'tp')
- new_v: bfloat16 [4, 8192, 1024], P(None, 'seq', 'tp')
The draws below stay inside these ranges and needn't reach their ends.
Inputs may be any that keep to these rules, and one draw needn't show every extreme that they name: `lengths`: some request has exactly 8184 valid positions. `migrating`: exactly 2 entries are 1. parents[r, 0] = -1 and 0 <= parents[r, i] < i for i >= 1. `accepted`: each row starts with node 0, each further entry's parent is the entry before it, 1 to 8 entries are nodes and the rest are -1; some row has 8 nodes.
All inputs are finite; a program needn't handle non-finite values.
Results may differ from the reference program's by a relative error of at most 0.015.
Values may be sent and summed in bfloat16 or wider, within the bound.
No kernel may reach another device: no remote copies, remote signals or barrier semaphores. Data moves between devices by JAX's collectives and lax.ppermute only.
A program may use at most 128 MiB of HBM per device.

```python
import math
import jax
import jax.numpy as jnp
from jax import lax

D = 4096
H = 32
KV = 8
HD = 128
REQS = 4
CACHE_DEV = 1024
DRAFTS = 64
ACCEPT_MAX = 8
CACHE_LEN = 8192
N_SEQ = 8


def tree_parts(key):
    base = jax.random.fold_in(key, 41)
    key_one, key_two, key_three, key_four = jax.random.split(base, 4)
    node = jnp.arange(DRAFTS, dtype=jnp.int32)
    chain = jax.random.randint(key_one, (REQS, DRAFTS), 0, 2)
    anywhere = jax.random.randint(key_two, (REQS, DRAFTS), 0, jnp.maximum(node, 1)[None, :])
    parents = jnp.where(chain == 1, node[None, :] - 1, anywhere)
    special = jax.random.randint(key_three, (), 0, REQS)
    request = jnp.arange(REQS, dtype=jnp.int32)[:, None]
    first = DRAFTS - ACCEPT_MAX + 1
    forced = jnp.where(node == first, 0, node - 1)[None, :]
    parents = jnp.where((request == special) & (node[None, :] >= first), forced, parents)
    parents = jnp.where(node[None, :] == 0, -1, parents).astype(jnp.int32)
    chosen = jax.random.randint(key_four, (REQS,), 0, DRAFTS)
    chosen = jnp.where(jnp.arange(REQS) == special, DRAFTS - 1, chosen).astype(jnp.int32)
    current = chosen
    trail = []
    for step in range(DRAFTS):
        trail.append(current)
        upward = jnp.take_along_axis(parents, jnp.maximum(current, 0)[:, None], axis=1)[:, 0]
        current = jnp.where(current > 0, upward, -1).astype(jnp.int32)
    trail = jnp.stack(trail, axis=1)
    count = jnp.sum((trail >= 0).astype(jnp.int32), axis=1)
    taken = jnp.minimum(count, ACCEPT_MAX)
    steps_in = jnp.arange(ACCEPT_MAX, dtype=jnp.int32)[None, :]
    index = jnp.clip(count[:, None] - 1 - steps_in, 0, DRAFTS - 1)
    path = jnp.take_along_axis(trail, index, axis=1)
    accepted = jnp.where(steps_in < taken[:, None], path, -1).astype(jnp.int32)
    return (parents, accepted)


def draw_parents(key, part):
    return tree_parts(key)[0]


def draw_accepted(key, part):
    return tree_parts(key)[1]


def draw_lengths(key, part):
    base = jax.random.fold_in(key, 21)
    key_one, key_two = jax.random.split(base, 2)
    drawn = jax.random.randint(key_one, (REQS,), 2, CACHE_LEN - ACCEPT_MAX + 1)
    special = jax.random.randint(key_two, (), 0, REQS)
    return jnp.where(jnp.arange(REQS) == special, CACHE_LEN - ACCEPT_MAX, drawn).astype(jnp.int32)


def draw_migrating(key, part):
    order = jax.random.permutation(jax.random.fold_in(key, 22), REQS)
    return (order < REQS // 2).astype(jnp.int32)


def float_parts(key):
    base = jax.random.fold_in(key, 51)
    keys = jax.random.split(base, 6)
    width = KV * HD
    head = jnp.clip(jax.random.normal(keys[0], (REQS, 2, width), jnp.float32), -5.0, 5.0)
    entries = jnp.clip(jax.random.normal(keys[1], (REQS * DRAFTS, H * HD), jnp.float32), -5.0, 5.0)
    return (head, entries, keys)


def draw_cache_k(key, part):
    head, entries, keys = float_parts(key)
    rest = jnp.clip(jax.random.normal(keys[2], (REQS, CACHE_LEN - 2, KV * HD), jnp.float32), -5.0, 5.0)
    return jnp.concatenate([head, rest], axis=1).astype(jnp.bfloat16)


def draw_draft_q(key, part):
    head, entries, keys = float_parts(key)
    return entries.astype(jnp.bfloat16)


def draw_draft_k(key, part):
    head, entries, keys = float_parts(key)
    own = 2.5 * jnp.mean(entries.reshape(REQS * DRAFTS, KV, H // KV, HD), axis=2).reshape(REQS * DRAFTS, KV * HD)
    noise = jnp.clip(jax.random.normal(keys[4], (REQS * DRAFTS, KV * HD), jnp.float32), -5.0, 5.0)
    return (own + noise).astype(jnp.bfloat16)


def block_scale(stream_key, dims, cuts, smallest, high):
    def one(dim, shards_of):
        draws = jax.random.uniform(jax.random.fold_in(jax.random.fold_in(stream_key, 6), dim), (shards_of,), jnp.float32, smallest / len(cuts), high / len(cuts))
        return jnp.repeat(jnp.exp(draws), dims[dim] // shards_of).reshape((-1,) + (1,) * (len(dims) - dim - 1))

    loudness = one(*cuts[0])
    for cut in cuts[1:]:
        loudness = loudness * one(*cut)
    return loudness


def gaussian(key, extent, scale, limit, cuts=(), kind=jnp.bfloat16):
    values = jax.random.normal(key, extent, jnp.float32) * scale
    if len(cuts) > 0:
        values = block_scale(key, extent, cuts, -0.22, 0.18) * values
    return jnp.clip(values, min=-limit, max=limit).astype(kind)


def setup_inputs(seed: int = 0) -> dict:
    seeds = jax.random.split(jax.random.key(seed), 11)
    draft_q = draw_draft_q(jax.random.fold_in(seeds[10], 71), 0)
    draft_k = draw_draft_k(jax.random.fold_in(seeds[10], 71), 0)
    draft_v = gaussian(seeds[2], (REQS * DRAFTS, KV * HD), 1.0, 6.0, ((0, 8), (1, 4)))
    cache_k = draw_cache_k(jax.random.fold_in(seeds[10], 71), 0)
    cache_v = gaussian(seeds[4], (REQS, CACHE_LEN, KV * HD), 1.0, 6.0, ((1, 8), (2, 4)))
    lengths = draw_lengths(jax.random.fold_in(seeds[10], 71), 0)
    migrating = draw_migrating(jax.random.fold_in(seeds[10], 71), 0)
    parents = draw_parents(jax.random.fold_in(seeds[10], 71), 0)
    accepted = draw_accepted(jax.random.fold_in(seeds[10], 71), 0)
    out_weight = gaussian(seeds[9], (D, D), D ** -0.5, 0.09375, ((0, 4),))
    return dict(draft_q=draft_q, draft_k=draft_k, draft_v=draft_v, cache_k=cache_k, cache_v=cache_v, lengths=lengths, migrating=migrating, parents=parents, accepted=accepted, out_weight=out_weight)


def ancestry(parents):
    count = parents.shape[1]
    node = jnp.arange(count, dtype=jnp.int32)
    anc = ((node[None, :, None] == node[None, None, :]) | (parents[:, :, None] == node[None, None, :])).astype(jnp.float32)
    for step in range(max(1, (count - 1).bit_length())):
        reach = jnp.einsum('rij,rjk->rik', anc, anc, precision=lax.Precision.HIGHEST)
        anc = jnp.where(anc + reach > 0.5, 1.0, 0.0).astype(jnp.float32)
    return anc

def reference(draft_q, draft_k, draft_v, cache_k, cache_v, lengths, migrating, parents, accepted, out_weight):
    width = KV * HD
    group = H // KV
    block = CACHE_DEV // N_SEQ
    scale = 1.0 / math.sqrt(HD)

    def arrange(cache):
        flipped = cache.reshape(REQS, N_SEQ, N_SEQ, block, width).swapaxes(1, 2).reshape(REQS, CACHE_LEN, width)
        return jnp.where((migrating == 1)[:, None, None], flipped, cache)
    canon_k = arrange(cache_k)
    canon_v = arrange(cache_v)
    anc = ancestry(parents)
    position = jnp.arange(CACHE_LEN, dtype=jnp.int32)

    def attend(request):
        start = (request * DRAFTS).astype(jnp.int32)
        rows = lax.dynamic_slice_in_dim(draft_q, start, DRAFTS, 0).astype(jnp.float32).reshape(DRAFTS, KV, group, HD)
        keys = lax.dynamic_index_in_dim(canon_k, request, 0, keepdims=False).astype(jnp.float32).reshape(CACHE_LEN, KV, HD)
        values = lax.dynamic_index_in_dim(canon_v, request, 0, keepdims=False).astype(jnp.float32).reshape(CACHE_LEN, KV, HD)
        dkeys = lax.dynamic_slice_in_dim(draft_k, start, DRAFTS, 0).astype(jnp.float32).reshape(DRAFTS, KV, HD)
        dvalues = lax.dynamic_slice_in_dim(draft_v, start, DRAFTS, 0).astype(jnp.float32).reshape(DRAFTS, KV, HD)
        live = position < lengths[request]
        tree = lax.dynamic_index_in_dim(anc, request, 0, keepdims=False) > 0.5
        cached = jnp.einsum('qkgd,pkd->kgqp', rows, keys, precision=lax.Precision.HIGHEST) * scale
        cached = jnp.where(live, cached, -1e+30)
        drafted = jnp.einsum('qkgd,pkd->kgqp', rows, dkeys, precision=lax.Precision.HIGHEST) * scale
        drafted = jnp.where(tree[None, None], drafted, -1e+30)
        top = jnp.maximum(lax.optimization_barrier(jnp.max(cached, axis=-1)), lax.optimization_barrier(jnp.max(drafted, axis=-1)))
        cache_w = jnp.where(live, jnp.exp(cached - top[..., None]), 0.0)
        draft_w = jnp.where(tree[None, None], jnp.exp(drafted - top[..., None]), 0.0)
        total = lax.optimization_barrier(jnp.sum(cache_w, axis=-1)) + lax.optimization_barrier(jnp.sum(draft_w, axis=-1))
        cache_r = lax.optimization_barrier(cache_w.astype(jnp.bfloat16)).astype(jnp.float32)
        draft_r = lax.optimization_barrier(draft_w.astype(jnp.bfloat16)).astype(jnp.float32)
        summed = jnp.einsum('kgqp,pkd->qkgd', cache_r, values, precision=lax.Precision.HIGHEST)
        summed = summed + jnp.einsum('kgqp,pkd->qkgd', draft_r, dvalues, precision=lax.Precision.HIGHEST)
        result = summed / jnp.transpose(total, (2, 0, 1))[..., None]
        return result.reshape(DRAFTS, D).astype(jnp.bfloat16)
    attention = lax.map(attend, jnp.arange(REQS, dtype=jnp.int32)).reshape(REQS * DRAFTS, D)
    attn_out = jnp.dot(attention, out_weight, preferred_element_type=jnp.float32).astype(jnp.bfloat16)
    valid = accepted >= 0
    node = jnp.maximum(accepted, 0).astype(jnp.int32)
    slot = lengths[:, None] + jnp.arange(ACCEPT_MAX, dtype=jnp.int32)[None, :]
    slot = jnp.where(valid, slot, CACHE_LEN).astype(jnp.int32)
    request_index = jnp.broadcast_to(jnp.arange(REQS, dtype=jnp.int32)[:, None], slot.shape)
    rows_k = jnp.take_along_axis(draft_k.reshape(REQS, DRAFTS, width), node[..., None], axis=1)
    rows_v = jnp.take_along_axis(draft_v.reshape(REQS, DRAFTS, width), node[..., None], axis=1)
    new_k = canon_k.at[request_index, slot].set(rows_k, mode='drop')
    new_v = canon_v.at[request_index, slot].set(rows_v, mode='drop')
    return (attn_out, new_k, new_v)
```

```python
import functools
import math

import jax
import jax.numpy as jnp
from jax import lax
from jax.experimental import pallas as pl
from jax.experimental.pallas import tpu as pltpu
from jax.sharding import PartitionSpec as P

HD = 128
NEG = -1e30
FLOOR = -1e20
STATS = 128
bf16 = jnp.bfloat16
f32 = jnp.float32
i32 = jnp.int32


def nt(a, b):
    return lax.dot_general(a, b, (((1,), (1,)), ((), ())), preferred_element_type=f32)


def tn(a, b):
    return lax.dot_general(a, b, (((0,), (0,)), ((), ())), preferred_element_type=f32)


def split3(x):
    hi = x.astype(bf16).astype(f32)
    rest = x - hi
    mid = rest.astype(bf16).astype(f32)
    return hi, mid, rest - mid


def migrating_pair(mig_ref, requests):
    first = i32(requests)
    last = i32(0)
    for r in reversed(range(requests)):
        first = jnp.where(mig_ref[r] == 1, r, first)
    for r in range(requests):
        last = jnp.where(mig_ref[r] == 1, r, last)
    return first, last


def prep_kernel(me_ref, mig_ref, parents_ref, accepted_ref, dk_ref, dv_ref, ck_ref, cv_ref, *rest, count, block):
    sends = rest[: count - 1]
    bias_ref, acc_ref, rows_ref, sems, acc_sem = rest[count - 1 :]
    requests, drafts = parents_ref.shape
    rows = dk_ref.shape[0]
    accept = accepted_ref.shape[1]
    me = me_ref[0]
    pair = migrating_pair(mig_ref, requests)
    copies = []
    for d in range(1, count):
        target = lax.rem(me + d, count)
        for c, cache in enumerate((ck_ref, cv_ref)):
            for m in range(2):
                copies.append(
                    pltpu.make_async_copy(
                        cache.at[pair[m], pl.ds(pl.multiple_of(target * block, block), block)],
                        sends[d - 1].at[pl.ds((2 * c + m) * block, block)],
                        sems.at[len(copies)],
                    )
                )
                copies[-1].start()
    request = (me * rows) // drafts
    offset = me * rows - request * drafts
    mine = lax.broadcasted_iota(i32, (requests, drafts), 0) == request
    parent = jnp.sum(jnp.where(mine, parents_ref[...], 0), axis=0, keepdims=True)
    down = lax.broadcasted_iota(i32, (drafts, drafts), 0)
    along = lax.broadcasted_iota(i32, (drafts, drafts), 1)
    reach = jnp.where((down == along) | (parent == down), 1.0, 0.0).astype(bf16)
    for _ in range(max(1, (drafts - 1).bit_length())):
        both = jnp.dot(reach, reach, preferred_element_type=f32)
        reach = jnp.where(both > 0.5, 1.0, 0.0).astype(bf16)
    pick = jnp.where(
        lax.broadcasted_iota(i32, (drafts, rows), 0) == lax.broadcasted_iota(i32, (drafts, rows), 1) + offset, 1.0, 0.0
    ).astype(bf16)
    bias_ref[...] = jnp.where(tn(reach, pick) > 0.5, 0.0, NEG)
    mine = lax.broadcasted_iota(i32, (requests, accept), 0) == request
    node = jnp.sum(jnp.where(mine, accepted_ref[...], 0), axis=0, keepdims=True)
    pick = jnp.where(lax.broadcasted_iota(i32, (rows, accept), 0) + offset == node, 1.0, 0.0).astype(bf16)
    chosen = jnp.concatenate([tn(pick, dk_ref[...]), tn(pick, dv_ref[...])], axis=0).astype(bf16)
    acc_ref[...] = chosen
    rows_ref[...] = chosen
    extra = []
    for d in range(1, count):
        extra.append(
            pltpu.make_async_copy(rows_ref, sends[d - 1].at[pl.ds(4 * block, 2 * accept)], acc_sem.at[d - 1])
        )
        extra[-1].start()
    for copy in copies + extra:
        copy.wait()


def attend_kernel(
    base_ref, me_ref, len_ref, mig_ref, *rest, half, count, block, group, drafted
):
    q_refs = rest[:half]
    k_ref, v_ref = rest[half : half + 2]
    rest = rest[half + 2 :]
    if drafted:
        dk_ref, dv_ref, bias_ref = rest[:3]
        rest = rest[3:]
    outs = rest[:half]
    q_all, part = rest[half:]
    step = pl.program_id(0)
    me = me_ref[0]
    spot = lax.rem(me, half)
    rows, q_width = q_refs[0].shape
    cache_dev = k_ref.shape[1]
    kv_local = k_ref.shape[2] // HD
    steps = pl.num_programs(0)
    per_request = q_all.shape[0] // 2
    drafts = per_request * rows
    heads = kv_local * group

    @pl.when(step == 0)
    def _():
        for e in range(half):
            q_all[lax.rem(spot + half - e, half)] = q_refs[e][...].astype(q_all.dtype)

    request = base_ref[0] + step
    row = lax.broadcasted_iota(i32, (1, cache_dev), 1)
    shift = block.bit_length() - 1
    moved = row + (row >> shift) * ((count - 1) * block) + me * block
    position = jnp.where(mig_ref[request] == 1, moved, row + me * cache_dev)
    dead = jnp.where(position < len_ref[request], 0.0, NEG)
    scale = math.log2(math.e) / math.sqrt(HD)
    rows_q = q_all[pl.ds(step * per_request, per_request)].reshape(drafts, q_width)
    tops, totals, sums = [], [], []
    for g in range(kv_local):
        q = jnp.concatenate(
            [rows_q[:, (g * group + j) * HD : (g * group + j + 1) * HD] for j in range(group)], axis=0
        ).astype(bf16)
        s = nt(q, k_ref[0, :, g * HD : (g + 1) * HD]) * scale + dead
        top = jnp.max(s, axis=1, keepdims=True)
        if drafted:
            own = jnp.where(request == (me * rows) // drafts, bias_ref[...], NEG)
            sd = nt(q, dk_ref[:, g * HD : (g + 1) * HD]) * scale + jnp.concatenate([own] * group, axis=0)
            top = jnp.maximum(top, jnp.max(sd, axis=1, keepdims=True))
        top = jnp.maximum(top, FLOOR)
        w = jnp.exp2(s - top)
        total = jnp.sum(w, axis=1, keepdims=True)
        o = jnp.dot(w.astype(bf16), v_ref[0, :, g * HD : (g + 1) * HD], preferred_element_type=f32)
        if drafted:
            wd = jnp.exp2(sd - top)
            total = total + jnp.sum(wd, axis=1, keepdims=True)
            o = o + jnp.dot(wd.astype(bf16), dv_ref[:, g * HD : (g + 1) * HD], preferred_element_type=f32)
        tops.append(top)
        totals.append(total)
        sums.append(o)
    lane = lax.broadcasted_iota(i32, (drafts, STATS), 1)
    stats = jnp.zeros((drafts, STATS), f32)
    for h in range(heads):
        g, j = divmod(h, group)
        at = slice(j * drafts, (j + 1) * drafts)
        values = split3(tops[g][at]) + split3(totals[g][at])[:2]
        for k, value in enumerate(values):
            stats = jnp.where(lane == k * heads + h, value, stats)
    for p in range(per_request):
        at = step * per_request + p
        for h in range(heads):
            g, j = divmod(h, group)
            part[at, :, h * HD : (h + 1) * HD] = sums[g][j * drafts + p * rows : j * drafts + (p + 1) * rows].astype(
                part.dtype
            )
        part[at, :, q_width:] = stats[p * rows : (p + 1) * rows].astype(part.dtype)

    @pl.when(step == steps - 1)
    def _():
        for e in range(half):
            outs[e][...] = part[lax.rem(spot + e, half)].astype(bf16)


def merge(parts, heads):
    width = heads * HD
    stats = [p[:, width:].astype(f32) for p in parts]
    tops = [
        s[:, :heads] + s[:, heads : 2 * heads] + s[:, 2 * heads : 3 * heads] for s in stats
    ]
    totals = [s[:, 3 * heads : 4 * heads] + s[:, 4 * heads : 5 * heads] for s in stats]
    top = functools.reduce(jnp.maximum, tops)
    factors = [jnp.exp2(t - top) for t in tops]
    total = sum(f * t for f, t in zip(factors, totals))
    sums = []
    for h in range(heads):
        sums.append(
            sum(
                f[:, h : h + 1] * p[:, h * HD : (h + 1) * HD].astype(f32) for f, p in zip(factors, parts)
            )
        )
    return top, total, sums


def reduce_kernel(*refs, heads):
    out = refs[-1]
    top, total, sums = merge([r[...] for r in refs[:-1]], heads)
    rows = out.shape[0]
    lane = lax.broadcasted_iota(i32, (rows, STATS), 1)
    stats = jnp.zeros((rows, STATS), f32)
    values = split3(top) + split3(total)[:2]
    for k, value in enumerate(values):
        for h in range(heads):
            stats = jnp.where(lane == k * heads + h, value[:, h : h + 1], stats)
    for h in range(heads):
        out[:, h * HD : (h + 1) * HD] = sums[h].astype(bf16)
    out[:, heads * HD :] = stats.astype(bf16)


def project_kernel(tp_ref, *refs, heads, ways):
    w_ref = refs[-ways - 1]
    parts = refs[: -ways - 1]
    outs = refs[-ways:-1]
    attention_ref = refs[-1]
    top, total, sums = merge([r[...] for r in parts], heads)
    width = w_ref.shape[1] // ways
    for h in range(heads):
        attention_ref[:, h * HD : (h + 1) * HD] = (sums[h] / total[:, h : h + 1]).astype(bf16)
    attention = attention_ref[...]
    for d in range(1, ways):
        target = lax.rem(tp_ref[0] + d, ways)
        w = w_ref[:, pl.ds(pl.multiple_of(target * width, width), width)]
        outs[d - 1][...] = jnp.dot(attention, w, preferred_element_type=f32).astype(bf16)


def finish_kernel(tp_ref, a_ref, w_ref, out_ref, *, ways):
    width = w_ref.shape[1] // ways
    w = w_ref[:, pl.ds(pl.multiple_of(tp_ref[0] * width, width), width)]
    out_ref[...] = jnp.dot(a_ref[...], w, preferred_element_type=f32)


def place_kernel(me_ref, mig_ref, len_ref, accepted_ref, acc_ref, ck_ref, cv_ref, *rest, count, block):
    gots = rest[: count - 1]
    nk_ref, nv_ref, rows_ref, wins_ref, sems, acc_sem, win_sem = rest[count - 1 :]
    requests, accept = accepted_ref.shape
    cache_dev = ck_ref.shape[1]
    me = me_ref[0]
    pair = migrating_pair(mig_ref, requests)
    stay = migrating_pair_other(mig_ref, requests)
    copies = []

    def go(src, dst):
        copies.append(pltpu.make_async_copy(src, dst, sems.at[len(copies)]))
        copies[-1].start()

    extra = [pltpu.make_async_copy(acc_ref, rows_ref.at[me], acc_sem.at[0])]
    extra[-1].start()
    for d in range(1, count):
        source = lax.rem(me + count - d, count)
        extra.append(
            pltpu.make_async_copy(gots[d - 1].at[pl.ds(4 * block, 2 * accept)], rows_ref.at[source], acc_sem.at[d])
        )
        extra[-1].start()
    at_me = pl.ds(pl.multiple_of(me * block, block), block)
    for c, (cache, new) in enumerate(((ck_ref, nk_ref), (cv_ref, nv_ref))):
        for m in range(2):
            go(cache.at[stay[m]], new.at[stay[m]])
            go(cache.at[pair[m], at_me], new.at[pair[m], at_me])
        for d in range(1, count):
            source = lax.rem(me + count - d, count)
            at = pl.ds(pl.multiple_of(source * block, block), block)
            for m in range(2):
                go(gots[d - 1].at[pl.ds((2 * c + m) * block, block)], new.at[pair[m], at])
    for copy in extra + copies:
        copy.wait()
    span = wins_ref.shape[2]
    first = [len_ref[r] - me * cache_dev for r in range(requests)]
    low = [
        pl.multiple_of(jnp.clip((x >> 4) << 4, 0, cache_dev - span), 16) for x in first
    ]
    loads, stores = [], []
    for c, new in enumerate((nk_ref, nv_ref)):
        for r in range(requests):
            a, b = new.at[r, pl.ds(low[r], span)], wins_ref.at[c, r]
            loads.append(pltpu.make_async_copy(a, b, win_sem.at[0, c, r]))
            stores.append(pltpu.make_async_copy(b, a, win_sem.at[1, c, r]))
    for copy in loads:
        copy.start()
    per_request = count // requests
    for copy in loads:
        copy.wait()
    for r in range(requests):
        held = rows_ref[r * per_request].astype(f32)
        for p in range(1, per_request):
            held = held + rows_ref[r * per_request + p].astype(f32)
        row = lax.broadcasted_iota(i32, (span, 1), 0) + low[r]
        for c in range(2):
            window = wins_ref[c, r].astype(f32)
            for i in range(accept):
                hit = (row == first[r] + i) & (accepted_ref[r, i] >= 0)
                window = jnp.where(hit, held[c * accept + i : c * accept + i + 1], window)
            wins_ref[c, r] = window.astype(bf16)
    for copy in stores:
        copy.start()
    for copy in stores:
        copy.wait()


def migrating_pair_other(mig_ref, requests):
    first = i32(requests)
    last = i32(0)
    for r in reversed(range(requests)):
        first = jnp.where(mig_ref[r] == 1, first, r)
    for r in range(requests):
        last = jnp.where(mig_ref[r] == 1, last, r)
    return first, last


SMEM = pl.BlockSpec(memory_space=pltpu.SMEM)
VMEM = pl.BlockSpec(memory_space=pltpu.VMEM)
ANY = pl.BlockSpec(memory_space=pl.ANY)
LIMIT = pltpu.CompilerParams(vmem_limit_bytes=48 << 20)


def per_device(
    draft_q, draft_k, draft_v, cache_k, cache_v, lengths, migrating, parents, accepted, out_weight
):
    count = lax.axis_size("seq")
    ways = lax.axis_size("tp")
    half = count // 2
    me = lax.axis_index("seq").astype(i32)
    tp = lax.axis_index("tp").astype(i32)
    rows, q_width = draft_q.shape
    requests, drafts = parents.shape
    accept = accepted.shape[1]
    cache_dev, kv_width = cache_k.shape[1:]
    group = q_width // kv_width
    heads = q_width // HD
    block = cache_dev // count
    me1 = me.reshape(1)
    tp1 = tp.reshape(1)
    across = [(i, (i + half) % count) for i in range(count)]
    beside = [
        [(i, i // half * half + (i + e) % half) for i in range(count)] for e in range(half)
    ]
    shifts = [[(i, (i + d) % count) for i in range(count)] for d in range(count)]
    turns = [[(i, (i + d) % ways) for i in range(ways)] for d in range(ways)]

    def to_mates(parts):
        return [lax.ppermute(parts[e], "seq", beside[e]) for e in range(1, half)]

    q_mirror = lax.ppermute(draft_q, "seq", across)
    q_mine = [draft_q] + to_mates([draft_q] * half)

    payload = 4 * block + 2 * accept
    prepared = pl.pallas_call(
        functools.partial(prep_kernel, count=count, block=block),
        out_shape=[jax.ShapeDtypeStruct((payload, kv_width), bf16)] * (count - 1)
        + [
            jax.ShapeDtypeStruct((drafts, rows), f32),
            jax.ShapeDtypeStruct((2 * accept, kv_width), bf16),
        ],
        in_specs=[SMEM, SMEM, VMEM, VMEM, VMEM, VMEM, ANY, ANY],
        out_specs=[ANY] * (count - 1) + [VMEM, VMEM],
        scratch_shapes=[
            pltpu.VMEM((2 * accept, kv_width), bf16),
            pltpu.SemaphoreType.DMA((4 * (count - 1),)),
            pltpu.SemaphoreType.DMA((count - 1,)),
        ],
        name="prep",
    )(me1, migrating, parents, accepted, draft_k, draft_v, cache_k, cache_v)
    sends, (bias, acc_rows) = prepared[: count - 1], prepared[count - 1 :]
    gots = [lax.ppermute(sends[d - 1], "seq", shifts[d]) for d in range(1, count)]

    q_theirs = [q_mirror] + to_mates([q_mirror] * half)

    def attend(queries, base, drafted):
        whole = lambda shape: pl.BlockSpec(shape, lambda r, *_: (0,) * len(shape))
        cache_spec = pl.BlockSpec((1, cache_dev, kv_width), lambda r, b, *_: (b[0] + r, 0, 0))
        operands = list(queries) + [cache_k, cache_v]
        specs = [whole((rows, q_width))] * half + [cache_spec] * 2
        if drafted:
            operands += [draft_k, draft_v, bias]
            specs += [whole((rows, kv_width))] * 2 + [whole((drafts, rows))]
        kind = bf16 if rows % 16 == 0 else f32
        return pl.pallas_call(
            functools.partial(
                attend_kernel, half=half, count=count, block=block, group=group, drafted=drafted
            ),
            out_shape=[jax.ShapeDtypeStruct((rows, q_width + STATS), bf16)] * half,
            grid_spec=pltpu.PrefetchScalarGridSpec(
                num_scalar_prefetch=4,
                grid=(requests // 2,),
                in_specs=specs,
                out_specs=[whole((rows, q_width + STATS))] * half,
                scratch_shapes=[
                    pltpu.VMEM((half, rows, q_width), kind),
                    pltpu.VMEM((half, rows, q_width + STATS), kind),
                ],
            ),
            compiler_params=LIMIT,
            name="attend_own" if drafted else "attend_other",
        )(base.reshape(1), me1, lengths, migrating, *operands)

    side = me // half
    mine = attend(q_mine, side * (requests // 2), True)
    theirs = attend(q_theirs, (1 - side) * (requests // 2), False)
    mine_got = to_mates(mine)
    theirs_got = to_mates(theirs)
    theirs_sum = pl.pallas_call(
        functools.partial(reduce_kernel, heads=heads),
        out_shape=jax.ShapeDtypeStruct((rows, q_width + STATS), bf16),
        in_specs=[VMEM] * half,
        out_specs=VMEM,
        name="reduce_other",
    )(theirs[0], *theirs_got)
    crossed = lax.ppermute(theirs_sum, "seq", across)
    width = out_weight.shape[1] // ways
    projected = pl.pallas_call(
        functools.partial(project_kernel, heads=heads, ways=ways),
        out_shape=[jax.ShapeDtypeStruct((rows, width), bf16)] * (ways - 1)
        + [jax.ShapeDtypeStruct((rows, q_width), bf16)],
        in_specs=[SMEM] + [VMEM] * (half + 2),
        out_specs=[VMEM] * ways,
        compiler_params=LIMIT,
        name="project",
    )(tp1, mine[0], *mine_got, crossed, out_weight)
    outs, attention = projected[:-1], projected[-1]
    out_got = [lax.ppermute(outs[d - 1], "tp", turns[d]) for d in range(1, ways)]
    own = pl.pallas_call(
        functools.partial(finish_kernel, ways=ways),
        out_shape=jax.ShapeDtypeStruct((rows, width), f32),
        in_specs=[SMEM, VMEM, VMEM],
        out_specs=VMEM,
        compiler_params=LIMIT,
        name="finish",
    )(tp1, attention, out_weight)
    attn_out = (own + sum(x.astype(f32) for x in out_got)).astype(bf16)

    span = 32
    new_k, new_v = pl.pallas_call(
        functools.partial(place_kernel, count=count, block=block),
        out_shape=[jax.ShapeDtypeStruct(cache_k.shape, bf16)] * 2,
        in_specs=[SMEM] * 4 + [ANY] * (count + 2),
        out_specs=[ANY, ANY],
        scratch_shapes=[
            pltpu.VMEM((count, 2 * accept, kv_width), bf16),
            pltpu.VMEM((2, requests, span, kv_width), bf16),
            pltpu.SemaphoreType.DMA((4 * (count + 1),)),
            pltpu.SemaphoreType.DMA((count,)),
            pltpu.SemaphoreType.DMA((2, 2, requests)),
        ],
        name="place",
    )(me1, migrating, lengths, accepted, acc_rows, cache_k, cache_v, *gots)
    return (attn_out, new_k, new_v)


def solution(mesh):
    in_specs = (
        P("seq", "tp"),
        P("seq", "tp"),
        P("seq", "tp"),
        P(None, "seq", "tp"),
        P(None, "seq", "tp"),
        P(),
        P(),
        P(),
        P(),
        P("tp", None),
    )
    out_specs = (P("seq", "tp"), P(None, "seq", "tp"), P(None, "seq", "tp"))
    return jax.shard_map(
        per_device, mesh=mesh, in_specs=in_specs, out_specs=out_specs, check_vma=False
    )
```

```python
import functools
import math

import jax
import jax.numpy as jnp
from jax import lax
from jax.experimental import pallas as pl
from jax.experimental.pallas import tpu as pltpu
from jax.sharding import PartitionSpec as P

HD = 128
NEG = -1e30
FLOOR = -1e20
STATS = 128
bf16 = jnp.bfloat16
f32 = jnp.float32
i32 = jnp.int32


def nt(a, b):
    return lax.dot_general(a, b, (((1,), (1,)), ((), ())), preferred_element_type=f32)


def tn(a, b):
    return lax.dot_general(a, b, (((0,), (0,)), ((), ())), preferred_element_type=f32)


def split3(x):
    hi = x.astype(bf16).astype(f32)
    rest = x - hi
    mid = rest.astype(bf16).astype(f32)
    return hi, mid, rest - mid


def migrating_pair(mig_ref, requests, flag=1):
    first = i32(0)
    last = i32(0)
    for r in reversed(range(requests)):
        first = jnp.where(mig_ref[r] == flag, r, first)
    for r in range(requests):
        last = jnp.where(mig_ref[r] == flag, r, last)
    return first, last


def block_copies(me, pair, caches, targets, slots, block, sems, back=False):
    copies = []
    for target, slot in zip(targets, slots):
        at = pl.ds(pl.multiple_of(target * block, block), block)
        for c, cache in enumerate(caches):
            for m in range(2):
                ends = cache.at[pair[m], at], slot.at[pl.ds((2 * c + m) * block, block)]
                copies.append(pltpu.make_async_copy(*(ends[::-1] if back else ends), sems.at[len(copies)]))
    return copies


def prep_kernel(me_ref, mig_ref, parents_ref, accepted_ref, dk_ref, dv_ref, ck_ref, cv_ref, near_ref, *rest, block):
    *outs, bias_ref, hold_ref, load_sems, store_sems, sems = rest
    half = near_ref.shape[0]
    requests, drafts = parents_ref.shape
    rows = dk_ref.shape[0]
    accept = accepted_ref.shape[1]
    me = me_ref[0]
    pair = migrating_pair(mig_ref, requests)
    caches = (ck_ref, cv_ref)
    mine = [me // half * half + t for t in range(half)]
    loads = block_copies(me, pair, caches, mine, [hold_ref.at[t] for t in range(half)], block, load_sems)
    copies = block_copies(me, pair, caches, [me ^ (half + n) for n in range(half)], outs, block, sems)
    for copy in loads + copies:
        copy.start()
    request = (me * rows) // drafts
    offset = me * rows - request * drafts
    mine = lax.broadcasted_iota(i32, (requests, drafts), 0) == request
    parent = jnp.sum(jnp.where(mine, parents_ref[...], 0), axis=0, keepdims=True)
    down = lax.broadcasted_iota(i32, (drafts, drafts), 0)
    along = lax.broadcasted_iota(i32, (drafts, drafts), 1)
    reach = jnp.where((down == along) | (parent == down), 1.0, 0.0).astype(bf16)
    for _ in range(max(1, (drafts - 1).bit_length())):
        both = jnp.dot(reach, reach, preferred_element_type=f32)
        reach = jnp.where(both > 0.5, 1.0, 0.0).astype(bf16)
    pick = jnp.where(
        lax.broadcasted_iota(i32, (drafts, rows), 0) == lax.broadcasted_iota(i32, (drafts, rows), 1) + offset, 1.0, 0.0
    ).astype(bf16)
    bias_ref[...] = jnp.where(tn(reach, pick) > 0.5, 0.0, NEG)
    mine = lax.broadcasted_iota(i32, (requests, accept), 0) == request
    node = jnp.sum(jnp.where(mine, accepted_ref[...], 0), axis=0, keepdims=True)
    pick = jnp.where(lax.broadcasted_iota(i32, (rows, accept), 0) + offset == node, 1.0, 0.0).astype(bf16)
    chosen = jnp.concatenate([tn(pick, dk_ref[...]), tn(pick, dv_ref[...])], axis=0).astype(bf16)
    for out in outs:
        out[4 * block :] = chosen
    stores = []
    for t in range(half):
        hold_ref[t, 4 * block :] = chosen
        for copy in loads[4 * t : 4 * t + 4]:
            copy.wait()
        stores.append(pltpu.make_async_copy(hold_ref.at[t], near_ref.at[t], store_sems.at[t]))
        stores[-1].start()
    for copy in stores + copies:
        copy.wait()


def attend_kernel(me_ref, len_ref, mig_ref, *rest, half, count, block, group, steps):
    q_refs = rest[:half]
    ck_ref, cv_ref, dk_ref, dv_ref, bias_ref = rest[half : half + 5]
    outs = rest[-half - 5 : -5]
    k_ref, v_ref, q_all, part, sems = rest[-5:]
    me = me_ref[0]
    spot = lax.rem(me, half)
    side = me // half
    rows, q_width = q_all.shape[2:]
    cache_dev = k_ref.shape[1]
    kv_local = k_ref.shape[2] // HD
    per_request = half // steps
    drafts = per_request * rows
    heads = kv_local * group
    requests = [side * steps + r for r in range(steps)] + [(1 - side) * steps + r for r in range(steps)]
    loads = []
    for i, request in enumerate(requests):
        for c, (cache, here) in enumerate(((ck_ref, k_ref), (cv_ref, v_ref))):
            loads.append(pltpu.make_async_copy(cache.at[request], here.at[i], sems.at[i, c]))
            loads[-1].start()
    for e in range(half):
        both = q_refs[e][...].astype(q_all.dtype)
        for k in range(2):
            q_all[k, spot ^ e] = both[k * rows : (k + 1) * rows]
    row = lax.broadcasted_iota(i32, (1, cache_dev), 1)
    shift = block.bit_length() - 1
    moved = row + (row >> shift) * ((count - 1) * block) + me * block
    scale = math.log2(math.e) / math.sqrt(HD)
    lane = lax.broadcasted_iota(i32, (drafts, STATS), 1)
    for i, request in enumerate(requests):
        drafted = i < steps
        k, step = divmod(i, steps)
        position = jnp.where(mig_ref[request] == 1, moved, row + me * cache_dev)
        dead = jnp.where(position < len_ref[request], 0.0, NEG)
        rows_q = q_all[k, step * per_request : (step + 1) * per_request].reshape(drafts, q_width)
        loads[2 * i].wait()
        loads[2 * i + 1].wait()
        stats = jnp.zeros((drafts, STATS), f32)
        for g in range(kv_local):
            at_g = slice(g * HD, (g + 1) * HD)
            q = jnp.concatenate(
                [rows_q[:, (g * group + j) * HD : (g * group + j + 1) * HD] for j in range(group)], axis=0
            ).astype(bf16)
            s = nt(q, k_ref[i, :, at_g]) * scale + dead
            top = jnp.max(s, axis=1, keepdims=True)
            if drafted:
                own = jnp.where(request == (me * rows) // drafts, bias_ref[...], NEG)
                sd = nt(q, dk_ref[:, at_g]) * scale + jnp.concatenate([own] * group, axis=0)
                top = jnp.maximum(top, jnp.max(sd, axis=1, keepdims=True))
            top = jnp.maximum(top, FLOOR)
            w = jnp.exp2(s - top)
            total = jnp.sum(w, axis=1, keepdims=True)
            o = jnp.dot(w.astype(bf16), v_ref[i, :, at_g], preferred_element_type=f32)
            if drafted:
                wd = jnp.exp2(sd - top)
                total = total + jnp.sum(wd, axis=1, keepdims=True)
                o = o + jnp.dot(wd.astype(bf16), dv_ref[:, at_g], preferred_element_type=f32)
            for j in range(group):
                h = g * group + j
                at = slice(j * drafts, (j + 1) * drafts)
                values = split3(top[at]) + split3(total[at])[:2]
                for n, value in enumerate(values):
                    stats = jnp.where(lane == n * heads + h, value, stats)
                for p in range(per_request):
                    part[k, step * per_request + p, :, h * HD : (h + 1) * HD] = o[
                        j * drafts + p * rows : j * drafts + (p + 1) * rows
                    ].astype(part.dtype)
        for p in range(per_request):
            part[k, step * per_request + p, :, q_width:] = stats[p * rows : (p + 1) * rows].astype(part.dtype)
    for e in range(half):
        outs[e][...] = jnp.concatenate([part[k, spot ^ e] for k in range(2)], axis=0).astype(bf16)


def view(ref, k, rows):
    def get(at):
        if rows % 16 == 0 or ref.shape[0] == rows:
            return ref[k * rows : (k + 1) * rows, at].astype(f32)
        return ref[:, at].astype(f32)[k * rows : (k + 1) * rows]

    return get


def merge(parts, heads):
    width = heads * HD
    stats = [get(slice(width, width + STATS)) for get in parts]
    tops = [s[:, :heads] + s[:, heads : 2 * heads] + s[:, 2 * heads : 3 * heads] for s in stats]
    totals = [s[:, 3 * heads : 4 * heads] + s[:, 4 * heads : 5 * heads] for s in stats]
    top = functools.reduce(jnp.maximum, tops)
    factors = [jnp.exp2(t - top) for t in tops]
    total = sum(f * t for f, t in zip(factors, totals))
    sums = []
    for h in range(heads):
        sums.append(sum(f[:, h : h + 1] * get(slice(h * HD, (h + 1) * HD)) for f, get in zip(factors, parts)))
    return top, total, sums


def reduce_kernel(*refs, heads):
    all_ref, out, sems = refs[-3:]
    rows = out.shape[0]
    top, total, sums = merge([view(r, 1, rows) for r in refs[:-3]], heads)
    lane = lax.broadcasted_iota(i32, (rows, STATS), 1)
    stats = jnp.zeros((rows, STATS), f32)
    values = split3(top) + split3(total)[:2]
    for k, value in enumerate(values):
        for h in range(heads):
            stats = jnp.where(lane == k * heads + h, value[:, h : h + 1], stats)
    for h in range(heads):
        out[:, h * HD : (h + 1) * HD] = sums[h].astype(bf16)
    out[:, heads * HD :] = stats.astype(bf16)
    copies = [pltpu.make_async_copy(out, all_ref.at[t], sems.at[t]) for t in range(2)]
    for copy in copies:
        copy.start()
    for copy in copies:
        copy.wait()


def weight_blocks(tp_ref, w_ref, here_ref, sems, targets):
    width = here_ref.shape[2]
    loads = []
    for n, target in enumerate(targets):
        at = pl.ds(pl.multiple_of((tp_ref[0] ^ target) * width, width), width)
        loads.append(pltpu.make_async_copy(w_ref.at[:, at], here_ref.at[n], sems.at[n]))
        loads[-1].start()
    return loads


def project_kernel(tp_ref, me_ref, done_ref, *refs, heads, targets):
    *parts, crossed_ref, w_ref, out_ref, attention_ref, here_ref, sems = refs
    width = here_ref.shape[2]
    loads = weight_blocks(tp_ref, w_ref, here_ref, sems, targets)
    rows = attention_ref.shape[0]
    other = 1 - me_ref[0] // len(parts)
    crossed = lambda at: crossed_ref[other, :, at].astype(f32)
    top, total, sums = merge([view(r, 0, rows) for r in parts] + [crossed], heads)
    for h in range(heads):
        attention_ref[:, h * HD : (h + 1) * HD] = (sums[h] / total[:, h : h + 1]).astype(bf16)
    attention = attention_ref[...]
    for n, load in enumerate(loads):
        load.wait()
        out_ref[:, n * width : (n + 1) * width] = jnp.dot(
            attention, here_ref[n], preferred_element_type=f32
        ).astype(bf16)


def finish_kernel(tp_ref, done_ref, a_ref, w_ref, *rest, targets):
    *outs, here_ref, sems = rest
    loads = weight_blocks(tp_ref, w_ref, here_ref, sems, targets)
    attention = a_ref[...]
    for n, load in enumerate(loads):
        load.wait()
        outs[n][...] = jnp.dot(attention, here_ref[n], preferred_element_type=f32)


def side_kernel(me_ref, mig_ref, ck_ref, cv_ref, after_ref, near_ref, *rest, which, block):
    gots = rest[: len(which)]
    nk_ref, nv_ref, done_ref, hold_ref, sems, near_sems, put_sems = rest[len(which) :]
    me = me_ref[0]
    half = near_ref.shape[0]
    stay = migrating_pair(mig_ref, ck_ref.shape[0], 0)
    pair = migrating_pair(mig_ref, ck_ref.shape[0])
    news = (nk_ref, nv_ref)
    loads, stores = [], []
    for c, cache in enumerate((ck_ref, cv_ref)):
        for m in range(2):
            loads.append(pltpu.make_async_copy(cache.at[stay[m]], hold_ref.at[c, m], sems.at[0, c, m]))
            stores.append(pltpu.make_async_copy(hold_ref.at[c, m], news[c].at[stay[m]], sems.at[1, c, m]))
    mine = [me // half * half + t for t in range(half)]
    copies = block_copies(me, pair, news, mine, [near_ref.at[t] for t in range(half)], block, near_sems, back=True)
    copies += block_copies(me, pair, news, [me ^ d for d in which], gots, block, put_sems, back=True)
    for copy in loads + copies:
        copy.start()
    done_ref[...] = jnp.zeros_like(done_ref)
    for load, store in zip(loads, stores):
        load.wait()
        store.start()
    for copy in stores + copies:
        copy.wait()


def put_kernel(me_ref, mig_ref, *rest, which, block):
    gots = rest[: len(which)]
    fk_ref, fv_ref, nk_ref, nv_ref, done_ref, sems = rest[len(which) :]
    pair = migrating_pair(mig_ref, mig_ref.shape[0])
    done_ref[...] = jnp.zeros_like(done_ref)
    me = me_ref[0]
    copies = block_copies(me, pair, (nk_ref, nv_ref), [me ^ d for d in which], gots, block, sems, back=True)
    for copy in copies:
        copy.start()
    for copy in copies:
        copy.wait()


def place_kernel(me_ref, mig_ref, len_ref, accepted_ref, near_ref, *rest, block):
    *gots, fk_ref, fv_ref, nk_ref, nv_ref, wins_ref, win_sem = rest
    requests, accept = accepted_ref.shape
    half = len(gots)
    count = 2 * half
    cache_dev = nk_ref.shape[1]
    me = me_ref[0]
    span = wins_ref.shape[2]
    first = [len_ref[r] - me * cache_dev for r in range(requests)]
    low = [pl.multiple_of(jnp.clip((x >> 4) << 4, 0, cache_dev - span), 16) for x in first]
    loads, stores = [], []
    for c, new in enumerate((nk_ref, nv_ref)):
        for r in range(requests):
            a, b = new.at[r, pl.ds(low[r], span)], wins_ref.at[c, r]
            loads.append(pltpu.make_async_copy(a, b, win_sem.at[0, c, r]))
            stores.append(pltpu.make_async_copy(b, a, win_sem.at[1, c, r]))
    for copy in loads:
        copy.start()
    per_request = count // requests
    for copy in loads:
        copy.wait()
    for r in range(requests):
        held = jnp.zeros((2 * accept, nk_ref.shape[2]), f32)
        for t in range(half):
            owner = me // half * half + t
            held = held + jnp.where(owner // per_request == r, near_ref[t, 4 * block :].astype(f32), 0.0)
        for n in range(half):
            owner = me ^ (half + n)
            held = held + jnp.where(owner // per_request == r, gots[n][4 * block :].astype(f32), 0.0)
        row = lax.broadcasted_iota(i32, (span, 1), 0) + low[r]
        for c in range(2):
            window = wins_ref[c, r].astype(f32)
            for i in range(accept):
                hit = (row == first[r] + i) & (accepted_ref[r, i] >= 0)
                window = jnp.where(hit, held[c * accept + i : c * accept + i + 1], window)
            wins_ref[c, r] = window.astype(bf16)
    for copy in stores:
        copy.start()
    for copy in stores:
        copy.wait()


SMEM = pl.BlockSpec(memory_space=pltpu.SMEM)
VMEM = pl.BlockSpec(memory_space=pltpu.VMEM)
HBM = pl.BlockSpec(memory_space=pltpu.HBM)

CHEAP = pl.CostEstimate(flops=1, transcendentals=0, bytes_accessed=1)


def limit(mib):
    return pltpu.CompilerParams(vmem_limit_bytes=mib << 20)


def per_device(
    draft_q, draft_k, draft_v, cache_k, cache_v, lengths, migrating, parents, accepted, out_weight
):
    count = lax.axis_size("seq")
    ways = lax.axis_size("tp")
    half = count // 2
    me = lax.axis_index("seq").astype(i32)
    tp = lax.axis_index("tp").astype(i32)
    rows, q_width = draft_q.shape
    requests, drafts = parents.shape
    accept = accepted.shape[1]
    cache_dev, kv_width = cache_k.shape[1:]
    group = q_width // kv_width
    heads = q_width // HD
    block = cache_dev // count
    draft_k, draft_v, cache_k, cache_v, lengths, migrating, parents, accepted, out_weight = [
        pltpu.with_memory_space_constraint(x, pltpu.HBM)
        for x in (draft_k, draft_v, cache_k, cache_v, lengths, migrating, parents, accepted, out_weight)
    ]
    me1 = me.reshape(1)
    tp1 = tp.reshape(1)
    across = [(i, (i + half) % count) for i in range(count)]
    beside = [[(i, i ^ e) for i in range(count)] for e in range(half)]

    def to_mates(parts):
        return [lax.ppermute(parts[e], "seq", beside[e]) for e in range(1, half)]

    q_mirror = lax.ppermute(draft_q, "seq", across)

    payload = 4 * block + 2 * accept
    near_send, *sends, bias = pl.pallas_call(
        functools.partial(prep_kernel, block=block),
        out_shape=[pltpu.HBM((half, payload, kv_width), bf16)]
        + [pltpu.VMEM((payload, kv_width), bf16)] * half
        + [pltpu.VMEM((drafts, rows), f32)],
        in_specs=[SMEM, SMEM, VMEM, VMEM, VMEM, VMEM, HBM, HBM],
        out_specs=[HBM] + [VMEM] * (half + 1),
        scratch_shapes=[
            pltpu.VMEM((half, payload, kv_width), bf16),
            pltpu.SemaphoreType.DMA((4 * half,)),
            pltpu.SemaphoreType.DMA((half,)),
            pltpu.SemaphoreType.DMA((4 * half,)),
        ],
        compiler_params=limit(4),
        cost_estimate=CHEAP,
        name="prep",
    )(me1, migrating, parents, accepted, draft_k, draft_v, cache_k, cache_v)
    sides = [list(range(k * half, (k + 1) * half)) for k in range(2)]
    q_mirror, sends = lax.optimization_barrier((q_mirror, sends))
    q_both = jnp.concatenate([draft_q, q_mirror], axis=0)
    q_got = to_mates([q_both] * half)
    near_send, _ = lax.optimization_barrier((near_send, q_got))
    near = lax.all_to_all(near_send, "seq", 0, 0, axis_index_groups=sides, tiled=True)
    gots = [None] * count

    def migrate(which, after):
        for d in which:
            send, _ = lax.optimization_barrier((sends[d - half], after))
            gots[d] = lax.ppermute(send, "seq", [(i, i ^ d) for i in range(count)])

    def part(which, k, n):
        which = list(which)
        return which[k * len(which) // n : (k + 1) * len(which) // n]

    groups = [part(range(half, count), k, 4) for k in range(4)]
    migrate(groups[0] + groups[1], q_got)
    steps = requests // 2
    kind = bf16 if rows % 16 == 0 else f32
    parts = pl.pallas_call(
        functools.partial(attend_kernel, half=half, count=count, block=block, group=group, steps=steps),
        out_shape=[pltpu.VMEM((2 * rows, q_width + STATS), bf16)] * half,
        in_specs=[SMEM] * 3 + [VMEM] * half + [HBM] * 2 + [VMEM] * 3,
        out_specs=[VMEM] * half,
        scratch_shapes=[
            pltpu.VMEM((2 * steps, cache_dev, kv_width), bf16),
            pltpu.VMEM((2 * steps, cache_dev, kv_width), bf16),
            pltpu.VMEM((2, half, rows, q_width), kind),
            pltpu.VMEM((2, half, rows, q_width + STATS), kind),
            pltpu.SemaphoreType.DMA((2 * steps, 2)),
        ],
        compiler_params=limit(20),
        cost_estimate=CHEAP,
        name="attend",
    )(me1, lengths, migrating, q_both, *q_got, cache_k, cache_v, draft_k, draft_v, bias)
    parts_got = to_mates(parts)
    shapes = [pltpu.HBM(cache_k.shape, bf16)] * 2
    token = pltpu.VMEM((8, 128), f32)

    def put(which, new_k, new_v):
        return pl.pallas_call(
            functools.partial(put_kernel, which=which, block=block),
            out_shape=shapes + [token],
            in_specs=[SMEM] * 2 + [VMEM] * len(which) + [HBM] * 2,
            out_specs=[HBM, HBM, VMEM],
            input_output_aliases={2 + len(which): 0, 3 + len(which): 1},
            scratch_shapes=[pltpu.SemaphoreType.DMA((4 * len(which),))],
            compiler_params=limit(2),
            cost_estimate=CHEAP,
            name="put",
        )(me1, migrating, *[gots[d] for d in which], new_k, new_v)

    migrate(groups[2], [gots[d] for d in groups[0]])
    early = groups[0] + groups[1]
    new_k, new_v, done = pl.pallas_call(
        functools.partial(side_kernel, which=early, block=block),
        out_shape=shapes + [token],
        in_specs=[SMEM, SMEM, HBM, HBM] + [VMEM] * (2 + len(early)),
        out_specs=[HBM, HBM, VMEM],
        scratch_shapes=[
            pltpu.VMEM((2, 2, cache_dev, kv_width), bf16),
            pltpu.SemaphoreType.DMA((2, 2, 2)),
            pltpu.SemaphoreType.DMA((4 * half,)),
            pltpu.SemaphoreType.DMA((4 * len(early),)),
        ],
        compiler_params=limit(4),
        cost_estimate=CHEAP,
        name="side",
    )(me1, migrating, cache_k, cache_v, parts[0], near, *[gots[d] for d in early])
    theirs_sum = pl.pallas_call(
        functools.partial(reduce_kernel, heads=heads),
        out_shape=pltpu.HBM((2, rows, q_width + STATS), bf16),
        in_specs=[VMEM] * half,
        out_specs=HBM,
        scratch_shapes=[pltpu.VMEM((rows, q_width + STATS), bf16), pltpu.SemaphoreType.DMA((2,))],
        compiler_params=limit(2),
        cost_estimate=CHEAP,
        name="reduce_other",
    )(*parts[:1], *parts_got)
    crossed = lax.all_to_all(
        theirs_sum, "seq", 0, 0, axis_index_groups=[[i, i + half] for i in range(half)], tiled=True
    )
    migrate(groups[3], theirs_sum)
    new_k, new_v, done = put(groups[2], new_k, new_v)
    width = out_weight.shape[1] // ways
    away, home = [t for t in range(ways) if t & 1], [t for t in range(ways) if not t & 1]
    blocks = lambda n: [pltpu.VMEM((n, q_width, width), bf16), pltpu.SemaphoreType.DMA((n,))]
    sent, attention = pl.pallas_call(
        functools.partial(project_kernel, heads=heads, targets=away),
        out_shape=[pltpu.VMEM((rows, len(away) * width), bf16), pltpu.VMEM((rows, q_width), bf16)],
        in_specs=[SMEM] * 2 + [VMEM] * (half + 2) + [HBM],
        out_specs=[VMEM] * 2,
        scratch_shapes=blocks(len(away)),
        compiler_params=limit(10),
        cost_estimate=CHEAP,
        name="project",
    )(tp1, me1, done, *parts[:1], *parts_got, crossed, out_weight)
    turn = lambda x, t: lax.ppermute(x, "tp", [(i, i ^ t) for i in range(ways)])
    came = turn(sent, 1).astype(f32)
    new_k, new_v, done = put(groups[3], new_k, new_v)
    own = pl.pallas_call(
        functools.partial(finish_kernel, targets=home),
        out_shape=[pltpu.VMEM((rows, width), f32)] * len(home),
        in_specs=[SMEM, VMEM, VMEM, HBM],
        out_specs=[VMEM] * len(home),
        scratch_shapes=blocks(len(home)),
        compiler_params=limit(10),
        cost_estimate=CHEAP,
        name="finish",
    )(tp1, done, attention, out_weight)
    held = {t: x + came[:, n * width : (n + 1) * width] for n, (t, x) in enumerate(zip(home, own))}
    step = 2
    while step < ways:
        leave = [t for t in held if t & step]
        came = turn(jnp.concatenate([held[t].astype(bf16) for t in leave], axis=1), step).astype(f32)
        held = {t ^ step: held[t ^ step] + came[:, n * width : (n + 1) * width] for n, t in enumerate(leave)}
        step *= 2
    attn_out = held[0].astype(bf16)

    span = 32
    new_k, new_v = pl.pallas_call(
        functools.partial(place_kernel, block=block),
        out_shape=shapes,
        in_specs=[SMEM] * 4 + [VMEM] * (1 + half) + [HBM, HBM],
        out_specs=[HBM, HBM],
        input_output_aliases={5 + half: 0, 6 + half: 1},
        scratch_shapes=[
            pltpu.VMEM((2, requests, span, kv_width), bf16),
            pltpu.SemaphoreType.DMA((2, 2, requests)),
        ],
        compiler_params=limit(4),
        cost_estimate=CHEAP,
        name="place",
    )(me1, migrating, lengths, accepted, near, *gots[half:], new_k, new_v)
    return (attn_out, new_k, new_v)


def solution(mesh):
    in_specs = (
        P("seq", "tp"),
        P("seq", "tp"),
        P("seq", "tp"),
        P(None, "seq", "tp"),
        P(None, "seq", "tp"),
        P(),
        P(),
        P(),
        P(),
        P("tp", None),
    )
    out_specs = (P("seq", "tp"), P(None, "seq", "tp"), P(None, "seq", "tp"))
    return jax.shard_map(
        per_device, mesh=mesh, in_specs=in_specs, out_specs=out_specs, check_vma=False
    )
```

```python
import functools
import math

import jax
import jax.numpy as jnp
from jax import lax
from jax.experimental import pallas as pl
from jax.experimental.pallas import tpu as pltpu
from jax.sharding import PartitionSpec as P

HD = 128
NEG = -1e30
FLOOR = -1e20
STATS = 128
bf16 = jnp.bfloat16
f32 = jnp.float32
i32 = jnp.int32


def nt(a, b):
    return lax.dot_general(a, b, (((1,), (1,)), ((), ())), preferred_element_type=f32)


def tn(a, b):
    return lax.dot_general(a, b, (((0,), (0,)), ((), ())), preferred_element_type=f32)


def split3(x):
    hi = x.astype(bf16).astype(f32)
    rest = x - hi
    mid = rest.astype(bf16).astype(f32)
    return hi, mid, rest - mid


def migrating_pair(mig_ref, requests, flag=1):
    first = i32(0)
    last = i32(0)
    for r in reversed(range(requests)):
        first = jnp.where(mig_ref[r] == flag, r, first)
    for r in range(requests):
        last = jnp.where(mig_ref[r] == flag, r, last)
    return first, last


def block_copies(me, pair, caches, targets, slots, block, sems, back=False):
    copies = []
    for target, slot in zip(targets, slots):
        at = pl.ds(pl.multiple_of(target * block, block), block)
        for c, cache in enumerate(caches):
            for m in range(2):
                ends = cache.at[pair[m], at], slot.at[pl.ds((2 * c + m) * block, block)]
                copies.append(pltpu.make_async_copy(*(ends[::-1] if back else ends), sems.at[len(copies)]))
    return copies


def deltas(me, kind, k, quarter):
    z = me // quarter
    inner = (z == 1) | (z == 2)
    pick = jnp.where if not isinstance(me, int) else lambda c, a, b: a if c else b
    near, far = quarter + k, 2 * quarter + k
    if kind == "inner":
        return pick(inner, far, near), pick(inner, near, far)
    if kind == "outer":
        return pick(inner, near, far), pick(inner, far, near)
    both = k if kind == "same" else 3 * quarter + k
    return both, both


def prep_kernel(me_ref, mig_ref, parents_ref, accepted_ref, dk_ref, dv_ref, ck_ref, cv_ref, *rest, ops, block, quarter):
    *outs, bias_ref, acc_ref, sems = rest
    requests, drafts = parents_ref.shape
    rows = dk_ref.shape[0]
    accept = accepted_ref.shape[1]
    me = me_ref[0]
    pair = migrating_pair(mig_ref, requests)
    goals = [me ^ deltas(me, kind, k, quarter)[0] for kind, k in ops]
    copies = block_copies(me, pair, (ck_ref, cv_ref), goals, outs, block, sems)
    for copy in copies:
        copy.start()
    request = (me * rows) // drafts
    offset = me * rows - request * drafts
    mine = lax.broadcasted_iota(i32, (requests, drafts), 0) == request
    parent = jnp.sum(jnp.where(mine, parents_ref[...], 0), axis=0, keepdims=True)
    down = lax.broadcasted_iota(i32, (drafts, drafts), 0)
    along = lax.broadcasted_iota(i32, (drafts, drafts), 1)
    reach = jnp.where((down == along) | (parent == down), 1.0, 0.0).astype(bf16)
    for _ in range(max(1, (drafts - 1).bit_length())):
        both = jnp.dot(reach, reach, preferred_element_type=f32)
        reach = jnp.where(both > 0.5, 1.0, 0.0).astype(bf16)
    pick = jnp.where(
        lax.broadcasted_iota(i32, (drafts, rows), 0) == lax.broadcasted_iota(i32, (drafts, rows), 1) + offset, 1.0, 0.0
    ).astype(bf16)
    bias_ref[...] = jnp.where(tn(reach, pick) > 0.5, 0.0, NEG)
    mine = lax.broadcasted_iota(i32, (requests, accept), 0) == request
    node = jnp.sum(jnp.where(mine, accepted_ref[...], 0), axis=0, keepdims=True)
    pick = jnp.where(lax.broadcasted_iota(i32, (rows, accept), 0) + offset == node, 1.0, 0.0).astype(bf16)
    chosen = jnp.concatenate([tn(pick, dk_ref[...]), tn(pick, dv_ref[...])], axis=0).astype(bf16)
    acc_ref[...] = chosen
    for out in outs:
        out[4 * block :] = chosen
    for copy in copies:
        copy.wait()


def attend_kernel(me_ref, len_ref, mig_ref, *rest, half, count, block, group, steps):
    q_refs = rest[:half]
    ck_ref, cv_ref, dk_ref, dv_ref, bias_ref = rest[half : half + 5]
    outs = rest[-half - 5 : -5]
    k_ref, v_ref, q_all, part, sems = rest[-5:]
    me = me_ref[0]
    spot = lax.rem(me, half)
    side = me // half
    rows, q_width = q_all.shape[2:]
    cache_dev = k_ref.shape[1]
    kv_local = k_ref.shape[2] // HD
    per_request = half // steps
    drafts = per_request * rows
    heads = kv_local * group
    requests = [side * steps + r for r in range(steps)] + [(1 - side) * steps + r for r in range(steps)]
    loads = []
    for i, request in enumerate(requests):
        for c, (cache, here) in enumerate(((ck_ref, k_ref), (cv_ref, v_ref))):
            loads.append(pltpu.make_async_copy(cache.at[request], here.at[i], sems.at[i, c]))
            loads[-1].start()
    for e in range(half):
        both = q_refs[e][...].astype(q_all.dtype)
        for k in range(2):
            q_all[k, spot ^ e] = both[k * rows : (k + 1) * rows]
    row = lax.broadcasted_iota(i32, (1, cache_dev), 1)
    shift = block.bit_length() - 1
    moved = row + (row >> shift) * ((count - 1) * block) + me * block
    scale = math.log2(math.e) / math.sqrt(HD)
    lane = lax.broadcasted_iota(i32, (drafts, STATS), 1)
    for i, request in enumerate(requests):
        drafted = i < steps
        k, step = divmod(i, steps)
        position = jnp.where(mig_ref[request] == 1, moved, row + me * cache_dev)
        dead = jnp.where(position < len_ref[request], 0.0, NEG)
        rows_q = q_all[k, step * per_request : (step + 1) * per_request].reshape(drafts, q_width)
        loads[2 * i].wait()
        loads[2 * i + 1].wait()
        stats = jnp.zeros((drafts, STATS), f32)
        for g in range(kv_local):
            at_g = slice(g * HD, (g + 1) * HD)
            q = jnp.concatenate(
                [rows_q[:, (g * group + j) * HD : (g * group + j + 1) * HD] for j in range(group)], axis=0
            ).astype(bf16)
            s = nt(q, k_ref[i, :, at_g]) * scale + dead
            top = jnp.max(s, axis=1, keepdims=True)
            if drafted:
                own = jnp.where(request == (me * rows) // drafts, bias_ref[...], NEG)
                sd = nt(q, dk_ref[:, at_g]) * scale + jnp.concatenate([own] * group, axis=0)
                top = jnp.maximum(top, jnp.max(sd, axis=1, keepdims=True))
            top = jnp.maximum(top, FLOOR)
            w = jnp.exp2(s - top)
            total = jnp.sum(w, axis=1, keepdims=True)
            o = jnp.dot(w.astype(bf16), v_ref[i, :, at_g], preferred_element_type=f32)
            if drafted:
                wd = jnp.exp2(sd - top)
                total = total + jnp.sum(wd, axis=1, keepdims=True)
                o = o + jnp.dot(wd.astype(bf16), dv_ref[:, at_g], preferred_element_type=f32)
            for j in range(group):
                h = g * group + j
                at = slice(j * drafts, (j + 1) * drafts)
                values = split3(top[at]) + split3(total[at])[:2]
                for n, value in enumerate(values):
                    stats = jnp.where(lane == n * heads + h, value, stats)
                for p in range(per_request):
                    part[k, step * per_request + p, :, h * HD : (h + 1) * HD] = o[
                        j * drafts + p * rows : j * drafts + (p + 1) * rows
                    ].astype(part.dtype)
        for p in range(per_request):
            part[k, step * per_request + p, :, q_width:] = stats[p * rows : (p + 1) * rows].astype(part.dtype)
    for e in range(half):
        outs[e][...] = jnp.concatenate([part[k, spot ^ e] for k in range(2)], axis=0).astype(bf16)


def view(ref, k, rows):
    def get(at):
        if rows % 16 == 0 or ref.shape[0] == rows:
            return ref[k * rows : (k + 1) * rows, at].astype(f32)
        return ref[:, at].astype(f32)[k * rows : (k + 1) * rows]

    return get


def merge(parts, heads):
    width = heads * HD
    stats = [get(slice(width, width + STATS)) for get in parts]
    tops = [s[:, :heads] + s[:, heads : 2 * heads] + s[:, 2 * heads : 3 * heads] for s in stats]
    totals = [s[:, 3 * heads : 4 * heads] + s[:, 4 * heads : 5 * heads] for s in stats]
    top = functools.reduce(jnp.maximum, tops)
    factors = [jnp.exp2(t - top) for t in tops]
    total = sum(f * t for f, t in zip(factors, totals))
    sums = []
    for h in range(heads):
        sums.append(sum(f[:, h : h + 1] * get(slice(h * HD, (h + 1) * HD)) for f, get in zip(factors, parts)))
    return top, total, sums


def reduce_kernel(*refs, heads):
    *parts, out = refs
    rows = out.shape[0]
    top, total, sums = merge([view(r, 1, rows) for r in parts], heads)
    lane = lax.broadcasted_iota(i32, (rows, STATS), 1)
    stats = jnp.zeros((rows, STATS), f32)
    values = split3(top) + split3(total)[:2]
    for k, value in enumerate(values):
        for h in range(heads):
            stats = jnp.where(lane == k * heads + h, value[:, h : h + 1], stats)
    for h in range(heads):
        out[:, h * HD : (h + 1) * HD] = sums[h].astype(bf16)
    out[:, heads * HD :] = stats.astype(bf16)


def project_kernel(tp_ref, done_ref, *refs, heads, ways):
    parts, w_ref, outs = refs[: -ways - 3], refs[-ways - 3], refs[-ways - 2 : -3]
    own_ref, here_ref, sems = refs[-3:]
    rows, width = own_ref.shape
    loads = []
    for d in range(ways):
        at = pl.ds(pl.multiple_of((tp_ref[0] ^ ((d + 1) % ways)) * width, width), width)
        loads.append(pltpu.make_async_copy(w_ref.at[:, at], here_ref.at[d], sems.at[d]))
        loads[-1].start()
    top, total, sums = merge([view(r, 0, rows) for r in parts], heads)
    attention = jnp.concatenate(
        [(sums[h] / total[:, h : h + 1]).astype(bf16) for h in range(heads)], axis=1
    )
    for d in range(ways):
        loads[d].wait()
        block = jnp.dot(attention, here_ref[d], preferred_element_type=f32)
        if d < ways - 1:
            outs[d][...] = block.astype(bf16)
        else:
            own_ref[...] = block


def final_kernel(done_ref, own_ref, *rest):
    out_ref = rest[-1]
    total = own_ref[...]
    for ref in rest[:-1]:
        total = total + ref[...].astype(f32)
    out_ref[...] = total.astype(bf16)


def put_kernel(me_ref, mig_ref, after_ref, *rest, ops, block, quarter, first, fill):
    gots = rest[: len(ops)]
    rest = rest[len(ops) :]
    if fill:
        ck_ref, cv_ref = rest[:2]
        rest = rest[2:]
    if not first:
        rest = rest[2:]
    nk_ref, nv_ref, done_ref, sems, *rest = rest
    me = me_ref[0]
    pair = migrating_pair(mig_ref, mig_ref.shape[0])
    news = (nk_ref, nv_ref)
    sources = [me ^ deltas(me, kind, k, quarter)[1] for kind, k in ops]
    copies = block_copies(me, pair, news, sources, gots, block, sems, back=True)
    for copy in copies:
        copy.start()
    done_ref[...] = jnp.zeros_like(done_ref)
    if fill:
        hold_ref, own_ref, hold_sems, own_sems = rest
        stay = migrating_pair(mig_ref, mig_ref.shape[0], 0)
        at = pl.ds(pl.multiple_of(me * block, block), block)
        loads, stores = [], []
        for c, (cache, new) in enumerate(zip((ck_ref, cv_ref), news)):
            for m in range(2):
                for here, held, there, sem in (
                    (cache.at[stay[m]], hold_ref.at[c, m], new.at[stay[m]], hold_sems),
                    (cache.at[pair[m], at], own_ref.at[c, m], new.at[pair[m], at], own_sems),
                ):
                    loads.append(pltpu.make_async_copy(here, held, sem.at[0, c, m]))
                    stores.append(pltpu.make_async_copy(held, there, sem.at[1, c, m]))
                    loads[-1].start()
        for load, store in zip(loads, stores):
            load.wait()
            store.start()
        copies = copies + stores
    for copy in copies:
        copy.wait()


def place_kernel(me_ref, mig_ref, len_ref, accepted_ref, acc_ref, *rest, ops, last, quarter, block):
    *gots, fk_ref, fv_ref, nk_ref, nv_ref, done_ref, wins_ref, sems, win_sem = rest
    requests, accept = accepted_ref.shape
    count = 4 * quarter
    cache_dev = nk_ref.shape[1]
    me = me_ref[0]
    pair = migrating_pair(mig_ref, requests)
    sources = [me ^ deltas(me, kind, k, quarter)[1] for kind, k in ops]
    done_ref[...] = jnp.zeros_like(done_ref)
    ends = [(source, got) for op, source, got in zip(ops, sources, gots) if op in last]
    copies = block_copies(me, pair, (nk_ref, nv_ref), *zip(*ends), block, sems, back=True)
    for copy in copies:
        copy.start()
    for copy in copies:
        copy.wait()
    span = wins_ref.shape[2]
    first = [len_ref[r] - me * cache_dev for r in range(requests)]
    low = [pl.multiple_of(jnp.clip((x >> 4) << 4, 0, cache_dev - span), 16) for x in first]
    loads, stores = [], []
    for c, new in enumerate((nk_ref, nv_ref)):
        for r in range(requests):
            a, b = new.at[r, pl.ds(low[r], span)], wins_ref.at[c, r]
            loads.append(pltpu.make_async_copy(a, b, win_sem.at[0, c, r]))
            stores.append(pltpu.make_async_copy(b, a, win_sem.at[1, c, r]))
    for copy in loads:
        copy.start()
    per_request = count // requests
    for copy in loads:
        copy.wait()
    for r in range(requests):
        held = jnp.where(me // per_request == r, acc_ref[...].astype(f32), 0.0)
        for owner, got in zip(sources, gots):
            held = held + jnp.where(owner // per_request == r, got[4 * block :].astype(f32), 0.0)
        row = lax.broadcasted_iota(i32, (span, 1), 0) + low[r]
        for c in range(2):
            window = wins_ref[c, r].astype(f32)
            for i in range(accept):
                hit = (row == first[r] + i) & (accepted_ref[r, i] >= 0)
                window = jnp.where(hit, held[c * accept + i : c * accept + i + 1], window)
            wins_ref[c, r] = window.astype(bf16)
    for copy in stores:
        copy.start()
    for copy in stores:
        copy.wait()


ANY = pl.BlockSpec(memory_space=pl.ANY)
SMEM = pl.BlockSpec(memory_space=pltpu.SMEM)
VMEM = pl.BlockSpec(memory_space=pltpu.VMEM)
HBM = pl.BlockSpec(memory_space=pltpu.HBM)

CHEAP = pl.CostEstimate(flops=1, transcendentals=0, bytes_accessed=1)


def limit(mib):
    return pltpu.CompilerParams(vmem_limit_bytes=mib << 20)


def per_device(
    draft_q, draft_k, draft_v, cache_k, cache_v, lengths, migrating, parents, accepted, out_weight
):
    count = lax.axis_size("seq")
    ways = lax.axis_size("tp")
    half = count // 2
    me = lax.axis_index("seq").astype(i32)
    tp = lax.axis_index("tp").astype(i32)
    rows, q_width = draft_q.shape
    requests, drafts = parents.shape
    accept = accepted.shape[1]
    cache_dev, kv_width = cache_k.shape[1:]
    group = q_width // kv_width
    heads = q_width // HD
    block = cache_dev // count
    draft_k, draft_v, cache_k, cache_v, lengths, migrating, parents, accepted, out_weight = [
        pltpu.with_memory_space_constraint(x, pltpu.HBM)
        for x in (draft_k, draft_v, cache_k, cache_v, lengths, migrating, parents, accepted, out_weight)
    ]
    me1 = me.reshape(1)
    tp1 = tp.reshape(1)
    across = [(i, (i + half) % count) for i in range(count)]
    beside = [[(i, i ^ e) for i in range(count)] for e in range(half)]

    def to_mates(parts):
        got = {e: lax.ppermute(parts[e], "seq", beside[e]) for e in reversed(range(1, half))}
        return [got[e] for e in range(1, half)]

    q_mirror = lax.ppermute(draft_q, "seq", across)

    payload = 4 * block + 2 * accept
    quarter = count // 4
    every = lambda kind, first=0: [(kind, k) for k in range(first, quarter)]
    bulk = every("inner") + every("outer") + every("same", 1) + every("across")
    *sends, bias, acc_rows = pl.pallas_call(
        functools.partial(prep_kernel, ops=bulk, block=block, quarter=quarter),
        out_shape=[pltpu.VMEM((payload, kv_width), bf16)] * len(bulk)
        + [pltpu.VMEM((drafts, rows), f32), pltpu.VMEM((2 * accept, kv_width), bf16)],
        in_specs=[SMEM, SMEM, VMEM, VMEM, VMEM, VMEM, HBM, HBM],
        out_specs=[VMEM] * (len(bulk) + 2),
        scratch_shapes=[pltpu.SemaphoreType.DMA((4 * len(bulk),))],
        compiler_params=limit(4),
        cost_estimate=CHEAP,
        name="prep",
    )(me1, migrating, parents, accepted, draft_k, draft_v, cache_k, cache_v)
    sends = dict(zip(bulk, sends))
    gots = {}

    def migrate(which, after):
        ready, after = lax.optimization_barrier(([sends[op] for op in which], after))
        for op, send in zip(which, ready):
            gots[op] = lax.ppermute(send, "seq", [(i, i ^ deltas(i, *op, quarter)[0]) for i in range(count)])
        return after

    q_mirror, bias = lax.optimization_barrier((q_mirror, bias))
    q_both = jnp.concatenate([draft_q, q_mirror], axis=0)
    q_got = to_mates([q_both] * half)
    far = every("across")
    draft_k = migrate(every("inner"), draft_k)
    q_got[0] = migrate(every("outer"), q_got[0])
    shapes = [pltpu.HBM(cache_k.shape, bf16)] * 2
    token = pltpu.VMEM((8, 128), f32)

    def put(which, filled, after, fill=False):
        pipes = [pltpu.SemaphoreType.DMA((4 * max(len(which), 1),))]
        if fill:
            pipes += [
                pltpu.VMEM((2, 2, cache_dev, kv_width), bf16),
                pltpu.VMEM((2, 2, block, kv_width), bf16),
                pltpu.SemaphoreType.DMA((2, 2, 2)),
                pltpu.SemaphoreType.DMA((2, 2, 2)),
            ]
        caches = [cache_k, cache_v] if fill else []
        base = 3 + len(which) + len(caches)
        return pl.pallas_call(
            functools.partial(put_kernel, ops=which, block=block, quarter=quarter, first=not filled, fill=fill),
            out_shape=shapes + [token],
            in_specs=[SMEM] * 2 + [ANY] + [VMEM] * len(which) + [HBM] * (len(caches) + len(filled)),
            out_specs=[HBM, HBM, VMEM],
            input_output_aliases={base: 0, base + 1: 1} if filled else {},
            scratch_shapes=pipes,
            compiler_params=limit(6),
            cost_estimate=CHEAP,
            name="put",
        )(me1, migrating, after, *[gots[op] for op in which], *caches, *filled)

    steps = requests // 2
    kind = bf16 if rows % 16 == 0 else f32
    parts = pl.pallas_call(
        functools.partial(attend_kernel, half=half, count=count, block=block, group=group, steps=steps),
        out_shape=[pltpu.VMEM((2 * rows, q_width + STATS), bf16)] * half,
        in_specs=[SMEM] * 3 + [VMEM] * half + [HBM] * 2 + [VMEM] * 3,
        out_specs=[VMEM] * half,
        scratch_shapes=[
            pltpu.VMEM((2 * steps, cache_dev, kv_width), bf16),
            pltpu.VMEM((2 * steps, cache_dev, kv_width), bf16),
            pltpu.VMEM((2, half, rows, q_width), kind),
            pltpu.VMEM((2, half, rows, q_width + STATS), kind),
            pltpu.SemaphoreType.DMA((2 * steps, 2)),
        ],
        compiler_params=limit(20),
        cost_estimate=CHEAP,
        name="attend",
    )(me1, lengths, migrating, q_both, *q_got, cache_k, cache_v, draft_k, draft_v, bias)
    *filled, done = put(every("inner"), [], parts[0])
    done = migrate(far[: quarter // 2], done)
    parts, done = lax.optimization_barrier((parts, done))
    parts_got = to_mates(parts)
    *filled, done = put(every("outer"), filled, done)
    done = migrate(far[quarter // 2 :], done)
    *filled, done = put(far[: quarter // 2], filled, done)
    done = migrate(every("same", 1), done)
    parts_got, done = lax.optimization_barrier((parts_got, done))
    theirs_sum = pl.pallas_call(
        functools.partial(reduce_kernel, heads=heads),
        out_shape=pltpu.VMEM((rows, q_width + STATS), bf16),
        in_specs=[VMEM] * half,
        out_specs=VMEM,
        compiler_params=limit(2),
        cost_estimate=CHEAP,
        name="reduce_other",
    )(parts[0], *parts_got)
    crossed = lax.ppermute(theirs_sum, "seq", across)
    theirs_sum, done = lax.optimization_barrier((theirs_sum, done))
    *filled, done = put([], filled, done, fill=True)
    last = far[quarter // 2 :] + every("same", 1)
    width = out_weight.shape[1] // ways
    *outs, own = pl.pallas_call(
        functools.partial(project_kernel, heads=heads, ways=ways),
        out_shape=[pltpu.VMEM((rows, width), bf16)] * (ways - 1) + [pltpu.VMEM((rows, width), f32)],
        in_specs=[SMEM] + [VMEM] * (half + 2) + [HBM],
        out_specs=[VMEM] * ways,
        scratch_shapes=[pltpu.VMEM((ways, q_width, width), bf16), pltpu.SemaphoreType.DMA((ways,))],
        compiler_params=limit(12),
        cost_estimate=CHEAP,
        name="project",
    )(tp1, done, parts[0], *parts_got, crossed, out_weight)
    out_got = [
        lax.ppermute(x, "tp", [(i, i ^ (d + 1)) for i in range(ways)]) for d, x in enumerate(outs)
    ]
    span = 32
    base = 5 + len(bulk)
    own, filled = lax.optimization_barrier((own, filled))
    new_k, new_v, done = pl.pallas_call(
        functools.partial(place_kernel, ops=bulk, last=last, quarter=quarter, block=block),
        out_shape=shapes + [token],
        in_specs=[SMEM] * 4 + [VMEM] * (1 + len(bulk)) + [HBM, HBM],
        out_specs=[HBM, HBM, VMEM],
        input_output_aliases={base: 0, base + 1: 1},
        scratch_shapes=[
            pltpu.VMEM((2, requests, span, kv_width), bf16),
            pltpu.SemaphoreType.DMA((4 * len(last),)),
            pltpu.SemaphoreType.DMA((2, 2, requests)),
        ],
        compiler_params=limit(4),
        cost_estimate=CHEAP,
        name="place",
    )(me1, migrating, lengths, accepted, acc_rows, *[gots[op] for op in bulk], *filled)
    attn_out = pl.pallas_call(
        final_kernel,
        out_shape=jax.ShapeDtypeStruct((rows, width), bf16),
        in_specs=[VMEM] * (1 + ways),
        out_specs=VMEM,
        compiler_params=limit(2),
        cost_estimate=CHEAP,
        name="final",
    )(done, own, *out_got)

    return (attn_out, new_k, new_v)


def solution(mesh):
    in_specs = (
        P("seq", "tp"),
        P("seq", "tp"),
        P("seq", "tp"),
        P(None, "seq", "tp"),
        P(None, "seq", "tp"),
        P(),
        P(),
        P(),
        P(),
        P("tp", None),
    )
    out_specs = (P("seq", "tp"), P(None, "seq", "tp"), P(None, "seq", "tp"))
    return jax.shard_map(
        per_device, mesh=mesh, in_specs=in_specs, out_specs=out_specs, check_vma=False
    )
```

```python
import functools
import math

import jax
import jax.numpy as jnp
from jax import lax
from jax.experimental import pallas as pl
from jax.experimental.pallas import tpu as pltpu
from jax.sharding import PartitionSpec as P

HD = 128
NEG = -1e30
FLOOR = -1e20
STATS = 128
bf16 = jnp.bfloat16
f32 = jnp.float32
i32 = jnp.int32


def nt(a, b):
    return lax.dot_general(a, b, (((1,), (1,)), ((), ())), preferred_element_type=f32)


def tn(a, b):
    return lax.dot_general(a, b, (((0,), (0,)), ((), ())), preferred_element_type=f32)


def split3(x):
    hi = x.astype(bf16).astype(f32)
    rest = x - hi
    mid = rest.astype(bf16).astype(f32)
    return hi, mid, rest - mid


def migrating_pair(mig_ref, requests, flag=1):
    first = i32(0)
    last = i32(0)
    for r in reversed(range(requests)):
        first = jnp.where(mig_ref[r] == flag, r, first)
    for r in range(requests):
        last = jnp.where(mig_ref[r] == flag, r, last)
    return first, last


def block_copies(me, pair, caches, targets, slots, block, sems, back=False):
    copies = []
    for target, slot in zip(targets, slots):
        at = pl.ds(pl.multiple_of(target * block, block), block)
        for c, cache in enumerate(caches):
            for m in range(2):
                ends = cache.at[pair[m], at], slot.at[pl.ds((2 * c + m) * block, block)]
                copies.append(pltpu.make_async_copy(*(ends[::-1] if back else ends), sems.at[len(copies)]))
    return copies


def deltas(me, kind, k, quarter):
    z = me // quarter
    inner = (z == 1) | (z == 2)
    pick = jnp.where if not isinstance(me, int) else lambda c, a, b: a if c else b
    near, far = quarter + k, 2 * quarter + k
    if kind == "inner":
        return pick(inner, far, near), pick(inner, near, far)
    if kind == "outer":
        return pick(inner, near, far), pick(inner, far, near)
    both = k if kind == "same" else 3 * quarter + k
    return both, both


def prep_kernel(me_ref, mig_ref, accepted_ref, dk_ref, dv_ref, ck_ref, cv_ref, *rest, ops, block, quarter):
    *outs, acc_ref, sems = rest
    requests, accept = accepted_ref.shape
    rows = dk_ref.shape[0]
    drafts = rows * quarter
    me = me_ref[0]
    pair = migrating_pair(mig_ref, requests)
    goals = [me ^ deltas(me, kind, k, quarter)[0] for kind, k in ops]
    copies = block_copies(me, pair, (ck_ref, cv_ref), goals, outs, block, sems)
    for copy in copies:
        copy.start()
    request = (me * rows) // drafts
    offset = me * rows - request * drafts
    mine = lax.broadcasted_iota(i32, (requests, accept), 0) == request
    node = jnp.sum(jnp.where(mine, accepted_ref[...], 0), axis=0, keepdims=True)
    pick = jnp.where(lax.broadcasted_iota(i32, (rows, accept), 0) + offset == node, 1.0, 0.0).astype(bf16)
    chosen = jnp.concatenate([tn(pick, dk_ref[...]), tn(pick, dv_ref[...])], axis=0).astype(bf16)
    acc_ref[...] = chosen
    for out in outs:
        out[4 * block :] = chosen
    for copy in copies:
        copy.wait()


def tree_bias(me_ref, parents_ref, rows):
    requests, drafts = parents_ref.shape
    request = (me_ref[0] * rows) // drafts
    offset = me_ref[0] * rows - request * drafts
    mine = lax.broadcasted_iota(i32, (requests, drafts), 0) == request
    parent = jnp.sum(jnp.where(mine, parents_ref[...], 0), axis=0, keepdims=True)
    down = lax.broadcasted_iota(i32, (drafts, drafts), 0)
    along = lax.broadcasted_iota(i32, (drafts, drafts), 1)
    reach = jnp.where((down == along) | (parent == down), 1.0, 0.0).astype(bf16)
    for _ in range(max(1, (drafts - 1).bit_length())):
        both = jnp.dot(reach, reach, preferred_element_type=f32)
        reach = jnp.where(both > 0.5, 1.0, 0.0).astype(bf16)
    pick = jnp.where(
        lax.broadcasted_iota(i32, (drafts, rows), 0) == lax.broadcasted_iota(i32, (drafts, rows), 1) + offset, 1.0, 0.0
    ).astype(bf16)
    return jnp.where(tn(reach, pick) > 0.5, 0.0, NEG)


def attend_kernel(me_ref, len_ref, mig_ref, *rest, count, block, group, own):
    quarter = count // 4
    q_refs = rest[:quarter]
    rest = rest[quarter:]
    if own:
        dk_ref, dv_ref, parents_ref = rest[:3]
        rest = rest[3:]
    ck_ref, cv_ref = rest[:2]
    outs = rest[2 : 2 + quarter]
    k_ref, v_ref, q_all, part, sems = rest[-5:]
    me = me_ref[0]
    spot = lax.rem(me, quarter)
    z = me // quarter
    first = z if own else z ^ 1
    rows, q_width = q_all.shape[2:]
    cache_dev = k_ref.shape[1]
    kv_local = k_ref.shape[2] // HD
    drafts = quarter * rows
    heads = kv_local * group
    requests = [first, first ^ 2]
    loads = []
    for i, request in enumerate(requests):
        for c, (cache, here) in enumerate(((ck_ref, k_ref), (cv_ref, v_ref))):
            loads.append(pltpu.make_async_copy(cache.at[request], here.at[i], sems.at[i, c]))
            loads[-1].start()
    for e in range(quarter):
        both = q_refs[e][...].astype(q_all.dtype)
        for k in range(2):
            q_all[k, spot ^ e] = both[k * rows : (k + 1) * rows]
    if own:
        bias = tree_bias(me_ref, parents_ref, rows)
    row = lax.broadcasted_iota(i32, (1, cache_dev), 1)
    shift = block.bit_length() - 1
    moved = row + (row >> shift) * ((count - 1) * block) + me * block
    scale = math.log2(math.e) / math.sqrt(HD)
    lane = lax.broadcasted_iota(i32, (drafts, STATS), 1)
    for i, request in enumerate(requests):
        drafted = own and i == 0
        position = jnp.where(mig_ref[request] == 1, moved, row + me * cache_dev)
        dead = jnp.where(position < len_ref[request], 0.0, NEG)
        rows_q = q_all[i].reshape(drafts, q_width)
        loads[2 * i].wait()
        loads[2 * i + 1].wait()
        stats = jnp.zeros((drafts, STATS), f32)
        for g in range(kv_local):
            at_g = slice(g * HD, (g + 1) * HD)
            q = jnp.concatenate(
                [rows_q[:, (g * group + j) * HD : (g * group + j + 1) * HD] for j in range(group)], axis=0
            ).astype(bf16)
            s = nt(q, k_ref[i, :, at_g]) * scale + dead
            top = jnp.max(s, axis=1, keepdims=True)
            if drafted:
                sd = nt(q, dk_ref[:, at_g]) * scale + jnp.concatenate([bias] * group, axis=0)
                top = jnp.maximum(top, jnp.max(sd, axis=1, keepdims=True))
            top = jnp.maximum(top, FLOOR)
            w = jnp.exp2(s - top)
            total = jnp.sum(w, axis=1, keepdims=True)
            o = jnp.dot(w.astype(bf16), v_ref[i, :, at_g], preferred_element_type=f32)
            if drafted:
                wd = jnp.exp2(sd - top)
                total = total + jnp.sum(wd, axis=1, keepdims=True)
                o = o + jnp.dot(wd.astype(bf16), dv_ref[:, at_g], preferred_element_type=f32)
            for j in range(group):
                h = g * group + j
                at = slice(j * drafts, (j + 1) * drafts)
                values = split3(top[at]) + split3(total[at])[:2]
                for n, value in enumerate(values):
                    stats = jnp.where(lane == n * heads + h, value, stats)
                for p in range(quarter):
                    part[i, p, :, h * HD : (h + 1) * HD] = o[
                        j * drafts + p * rows : j * drafts + (p + 1) * rows
                    ].astype(part.dtype)
        for p in range(quarter):
            part[i, p, :, q_width:] = stats[p * rows : (p + 1) * rows].astype(part.dtype)
    for e in range(quarter):
        outs[e][...] = jnp.concatenate([part[k, spot ^ e] for k in range(2)], axis=0).astype(bf16)


def view(ref, k, rows):
    def get(at):
        if rows % 16 == 0 or ref.shape[0] == rows:
            return ref[k * rows : (k + 1) * rows, at].astype(f32)
        return ref[:, at].astype(f32)[k * rows : (k + 1) * rows]

    return get


def merge(parts, heads):
    width = heads * HD
    stats = [get(slice(width, width + STATS)) for get in parts]
    tops = [s[:, :heads] + s[:, heads : 2 * heads] + s[:, 2 * heads : 3 * heads] for s in stats]
    totals = [s[:, 3 * heads : 4 * heads] + s[:, 4 * heads : 5 * heads] for s in stats]
    top = functools.reduce(jnp.maximum, tops)
    factors = [jnp.exp2(t - top) for t in tops]
    total = sum(f * t for f, t in zip(factors, totals))
    sums = []
    for h in range(heads):
        sums.append(sum(f[:, h : h + 1] * get(slice(h * HD, (h + 1) * HD)) for f, get in zip(factors, parts)))
    return top, total, sums


def reduce_kernel(*refs, heads):
    *parts, out = refs
    rows = out.shape[0]
    top, total, sums = merge([view(r, 1, rows) for r in parts], heads)
    lane = lax.broadcasted_iota(i32, (rows, STATS), 1)
    stats = jnp.zeros((rows, STATS), f32)
    values = split3(top) + split3(total)[:2]
    for k, value in enumerate(values):
        for h in range(heads):
            stats = jnp.where(lane == k * heads + h, value[:, h : h + 1], stats)
    for h in range(heads):
        out[:, h * HD : (h + 1) * HD] = sums[h].astype(bf16)
    out[:, heads * HD :] = stats.astype(bf16)


def weight_kernel(tp_ref, after_ref, w_ref, here_ref, sems):
    ways, _, width = here_ref.shape
    loads = []
    for d in range(ways):
        at = pl.ds(pl.multiple_of((tp_ref[0] ^ ((d + 1) % ways)) * width, width), width)
        loads.append(pltpu.make_async_copy(w_ref.at[:, at], here_ref.at[d], sems.at[d]))
        loads[-1].start()
    for load in loads:
        load.wait()


def project_kernel(done_ref, *refs, heads, ways):
    parts, here_ref, outs = refs[: -ways - 1], refs[-ways - 1], refs[-ways:-1]
    own_ref = refs[-1]
    rows, width = own_ref.shape
    top, total, sums = merge([view(r, 0, rows) for r in parts], heads)
    attention = jnp.concatenate(
        [(sums[h] / total[:, h : h + 1]).astype(bf16) for h in range(heads)], axis=1
    )
    for d in range(ways):
        block = jnp.dot(attention, here_ref[d], preferred_element_type=f32)
        if d < ways - 1:
            outs[d][...] = block.astype(bf16)
        else:
            own_ref[...] = block


def final_kernel(done_ref, own_ref, *rest):
    out_ref = rest[-1]
    total = own_ref[...]
    for ref in rest[:-1]:
        total = total + ref[...].astype(f32)
    out_ref[...] = total.astype(bf16)


def put_kernel(me_ref, mig_ref, after_ref, *rest, ops, block, quarter, first, fill):
    gots = rest[: len(ops)]
    rest = rest[len(ops) :]
    if fill:
        ck_ref, cv_ref = rest[:2]
        rest = rest[2:]
    if not first:
        rest = rest[2:]
    nk_ref, nv_ref, done_ref, sems, *rest = rest
    me = me_ref[0]
    pair = migrating_pair(mig_ref, mig_ref.shape[0])
    news = (nk_ref, nv_ref)
    sources = [me ^ deltas(me, kind, k, quarter)[1] for kind, k in ops]
    copies = block_copies(me, pair, news, sources, gots, block, sems, back=True)
    for copy in copies:
        copy.start()
    done_ref[...] = jnp.zeros_like(done_ref)
    if fill:
        hold_ref, own_ref, hold_sems, own_sems = rest
        stay = migrating_pair(mig_ref, mig_ref.shape[0], 0)
        at = pl.ds(pl.multiple_of(me * block, block), block)
        loads, stores = [], []
        for c, (cache, new) in enumerate(zip((ck_ref, cv_ref), news)):
            for m in range(2):
                for here, held, there, sem in (
                    (cache.at[stay[m]], hold_ref.at[c, m], new.at[stay[m]], hold_sems),
                    (cache.at[pair[m], at], own_ref.at[c, m], new.at[pair[m], at], own_sems),
                ):
                    loads.append(pltpu.make_async_copy(here, held, sem.at[0, c, m]))
                    stores.append(pltpu.make_async_copy(held, there, sem.at[1, c, m]))
                    loads[-1].start()
        for load, store in zip(loads, stores):
            load.wait()
            store.start()
        copies = copies + stores
    for copy in copies:
        copy.wait()


def place_kernel(me_ref, mig_ref, len_ref, accepted_ref, acc_ref, *rest, ops, last, quarter, block):
    *gots, fk_ref, fv_ref, nk_ref, nv_ref, done_ref, wins_ref, sems, win_sem = rest
    requests, accept = accepted_ref.shape
    count = 4 * quarter
    cache_dev = nk_ref.shape[1]
    me = me_ref[0]
    pair = migrating_pair(mig_ref, requests)
    sources = [me ^ deltas(me, kind, k, quarter)[1] for kind, k in ops]
    done_ref[...] = jnp.zeros_like(done_ref)
    ends = [(source, got) for op, source, got in zip(ops, sources, gots) if op in last]
    copies = block_copies(me, pair, (nk_ref, nv_ref), *zip(*ends), block, sems, back=True)
    for copy in copies:
        copy.start()
    for copy in copies:
        copy.wait()
    span = wins_ref.shape[2]
    first = [len_ref[r] - me * cache_dev for r in range(requests)]
    low = [pl.multiple_of(jnp.clip((x >> 4) << 4, 0, cache_dev - span), 16) for x in first]
    loads, stores = [], []
    for c, new in enumerate((nk_ref, nv_ref)):
        for r in range(requests):
            a, b = new.at[r, pl.ds(low[r], span)], wins_ref.at[c, r]
            loads.append(pltpu.make_async_copy(a, b, win_sem.at[0, c, r]))
            stores.append(pltpu.make_async_copy(b, a, win_sem.at[1, c, r]))
    for copy in loads:
        copy.start()
    per_request = count // requests
    for copy in loads:
        copy.wait()
    for r in range(requests):
        held = jnp.where(me // per_request == r, acc_ref[...].astype(f32), 0.0)
        for owner, got in zip(sources, gots):
            held = held + jnp.where(owner // per_request == r, got[4 * block :].astype(f32), 0.0)
        row = lax.broadcasted_iota(i32, (span, 1), 0) + low[r]
        for c in range(2):
            window = wins_ref[c, r].astype(f32)
            for i in range(accept):
                hit = (row == first[r] + i) & (accepted_ref[r, i] >= 0)
                window = jnp.where(hit, held[c * accept + i : c * accept + i + 1], window)
            wins_ref[c, r] = window.astype(bf16)
    for copy in stores:
        copy.start()
    for copy in stores:
        copy.wait()


ANY = pl.BlockSpec(memory_space=pl.ANY)
SMEM = pl.BlockSpec(memory_space=pltpu.SMEM)
VMEM = pl.BlockSpec(memory_space=pltpu.VMEM)
HBM = pl.BlockSpec(memory_space=pltpu.HBM)

CHEAP = pl.CostEstimate(flops=1, transcendentals=0, bytes_accessed=1)


def limit(mib):
    return pltpu.CompilerParams(vmem_limit_bytes=mib << 20)


def per_device(
    draft_q, draft_k, draft_v, cache_k, cache_v, lengths, migrating, parents, accepted, out_weight
):
    count = lax.axis_size("seq")
    ways = lax.axis_size("tp")
    half = count // 2
    me = lax.axis_index("seq").astype(i32)
    tp = lax.axis_index("tp").astype(i32)
    rows, q_width = draft_q.shape
    requests, drafts = parents.shape
    accept = accepted.shape[1]
    cache_dev, kv_width = cache_k.shape[1:]
    group = q_width // kv_width
    heads = q_width // HD
    block = cache_dev // count
    draft_k, draft_v, cache_k, cache_v, lengths, migrating, parents, accepted, out_weight = [
        pltpu.with_memory_space_constraint(x, pltpu.HBM)
        for x in (draft_k, draft_v, cache_k, cache_v, lengths, migrating, parents, accepted, out_weight)
    ]
    me1 = me.reshape(1)
    tp1 = tp.reshape(1)
    across = [(i, (i + half) % count) for i in range(count)]
    beside = [[(i, i ^ e) for i in range(count)] for e in range(half)]

    def to_mates(parts):
        got = {e: lax.ppermute(parts[e], "seq", beside[e]) for e in reversed(range(1, half))}
        return [got[e] for e in range(1, half)]

    q_mirror = lax.ppermute(draft_q, "seq", across)

    payload = 4 * block + 2 * accept
    quarter = count // 4
    every = lambda kind, first=0: [(kind, k) for k in range(first, quarter)]
    bulk = every("inner") + every("outer") + every("same", 1) + every("across")
    *sends, acc_rows = pl.pallas_call(
        functools.partial(prep_kernel, ops=bulk, block=block, quarter=quarter),
        out_shape=[pltpu.VMEM((payload, kv_width), bf16)] * len(bulk)
        + [pltpu.VMEM((2 * accept, kv_width), bf16)],
        in_specs=[SMEM, SMEM, VMEM, VMEM, VMEM, HBM, HBM],
        out_specs=[VMEM] * (len(bulk) + 1),
        scratch_shapes=[pltpu.SemaphoreType.DMA((4 * len(bulk),))],
        compiler_params=limit(4),
        cost_estimate=CHEAP,
        name="prep",
    )(me1, migrating, accepted, draft_k, draft_v, cache_k, cache_v)
    sends = dict(zip(bulk, sends))
    gots = {}

    def migrate(which, after):
        ready, after = lax.optimization_barrier(([sends[op] for op in which], after))
        for op, send in zip(which, ready):
            gots[op] = lax.ppermute(send, "seq", [(i, i ^ deltas(i, *op, quarter)[0]) for i in range(count)])
        return after

    q_mirror, acc_rows = lax.optimization_barrier((q_mirror, acc_rows))
    q_both = jnp.concatenate([draft_q, q_mirror], axis=0)
    q_got = to_mates([q_both] * half)
    far = every("across")
    draft_k = migrate(every("inner"), draft_k)
    q_got[0] = migrate(every("outer"), q_got[0])
    shapes = [pltpu.HBM(cache_k.shape, bf16)] * 2
    token = pltpu.VMEM((8, 128), f32)

    def put(which, filled, after, fill=False):
        pipes = [pltpu.SemaphoreType.DMA((4 * max(len(which), 1),))]
        if fill:
            pipes += [
                pltpu.VMEM((2, 2, cache_dev, kv_width), bf16),
                pltpu.VMEM((2, 2, block, kv_width), bf16),
                pltpu.SemaphoreType.DMA((2, 2, 2)),
                pltpu.SemaphoreType.DMA((2, 2, 2)),
            ]
        caches = [cache_k, cache_v] if fill else []
        base = 3 + len(which) + len(caches)
        return pl.pallas_call(
            functools.partial(put_kernel, ops=which, block=block, quarter=quarter, first=not filled, fill=fill),
            out_shape=shapes + [token],
            in_specs=[SMEM] * 2 + [ANY] + [VMEM] * len(which) + [HBM] * (len(caches) + len(filled)),
            out_specs=[HBM, HBM, VMEM],
            input_output_aliases={base: 0, base + 1: 1} if filled else {},
            scratch_shapes=pipes,
            compiler_params=limit(6),
            cost_estimate=CHEAP,
            name="put",
        )(me1, migrating, after, *[gots[op] for op in which], *caches, *filled)

    assert requests == 4 and drafts == quarter * rows
    kind = bf16 if rows % 16 == 0 else f32

    def attend(queries, own):
        drafted = [draft_k, draft_v, parents] if own else []
        return pl.pallas_call(
            functools.partial(attend_kernel, count=count, block=block, group=group, own=own),
            out_shape=[pltpu.VMEM((2 * rows, q_width + STATS), bf16)] * quarter,
            in_specs=[SMEM] * 3 + [VMEM] * (quarter + len(drafted)) + [HBM] * 2,
            out_specs=[VMEM] * quarter,
            scratch_shapes=[
                pltpu.VMEM((2, cache_dev, kv_width), bf16),
                pltpu.VMEM((2, cache_dev, kv_width), bf16),
                pltpu.VMEM((2, quarter, rows, q_width), kind),
                pltpu.VMEM((2, quarter, rows, q_width + STATS), kind),
                pltpu.SemaphoreType.DMA((2, 2)),
            ],
            compiler_params=limit(16),
            cost_estimate=CHEAP,
            name="attend_own" if own else "attend_next",
        )(me1, lengths, migrating, *queries, *drafted, cache_k, cache_v)

    q_all = [q_both] + q_got
    parts = attend(q_all[:quarter], True)
    q_next, parts = lax.optimization_barrier((q_all[quarter:], parts))
    later = attend(q_next, False)
    *filled, done = put(every("inner"), [], later[0])
    done = migrate(far[: quarter // 2], done)
    later, done = lax.optimization_barrier((later, done))
    parts = parts + later
    parts_got = to_mates(parts)
    *filled, done = put(every("outer"), filled, done)
    done = migrate(far[quarter // 2 :], done)
    *filled, done = put([], filled, done, fill=True)
    *filled, done = put(far[: quarter // 2], filled, done)
    done = migrate(every("same", 1), done)
    parts_got, done = lax.optimization_barrier((parts_got, done))
    theirs_sum = pl.pallas_call(
        functools.partial(reduce_kernel, heads=heads),
        out_shape=pltpu.VMEM((rows, q_width + STATS), bf16),
        in_specs=[VMEM] * half,
        out_specs=VMEM,
        compiler_params=limit(2),
        cost_estimate=CHEAP,
        name="reduce_other",
    )(parts[0], *parts_got)
    crossed = lax.ppermute(theirs_sum, "seq", across)
    last = far[quarter // 2 :] + every("same", 1)
    width = out_weight.shape[1] // ways
    weight = pl.pallas_call(
        weight_kernel,
        out_shape=pltpu.VMEM((ways, q_width, width), bf16),
        in_specs=[SMEM, ANY, HBM],
        out_specs=VMEM,
        scratch_shapes=[pltpu.SemaphoreType.DMA((ways,))],
        compiler_params=limit(1),
        cost_estimate=CHEAP,
        name="weight",
    )(tp1, theirs_sum, out_weight)
    weight, crossed = lax.optimization_barrier((weight, crossed))
    *outs, own = pl.pallas_call(
        functools.partial(project_kernel, heads=heads, ways=ways),
        out_shape=[pltpu.VMEM((rows, width), bf16)] * (ways - 1) + [pltpu.VMEM((rows, width), f32)],
        in_specs=[VMEM] * (half + 3),
        out_specs=[VMEM] * ways,
        compiler_params=limit(4),
        cost_estimate=CHEAP,
        name="project",
    )(done, parts[0], *parts_got, crossed, weight)
    out_got = [
        lax.ppermute(x, "tp", [(i, i ^ (d + 1)) for i in range(ways)]) for d, x in enumerate(outs)
    ]
    span = 32
    base = 5 + len(bulk)
    own, filled = lax.optimization_barrier((own, filled))
    new_k, new_v, done = pl.pallas_call(
        functools.partial(place_kernel, ops=bulk, last=last, quarter=quarter, block=block),
        out_shape=shapes + [token],
        in_specs=[SMEM] * 4 + [VMEM] * (1 + len(bulk)) + [HBM, HBM],
        out_specs=[HBM, HBM, VMEM],
        input_output_aliases={base: 0, base + 1: 1},
        scratch_shapes=[
            pltpu.VMEM((2, requests, span, kv_width), bf16),
            pltpu.SemaphoreType.DMA((4 * len(last),)),
            pltpu.SemaphoreType.DMA((2, 2, requests)),
        ],
        compiler_params=limit(4),
        cost_estimate=CHEAP,
        name="place",
    )(me1, migrating, lengths, accepted, acc_rows, *[gots[op] for op in bulk], *filled)
    attn_out = pl.pallas_call(
        final_kernel,
        out_shape=jax.ShapeDtypeStruct((rows, width), bf16),
        in_specs=[VMEM] * (1 + ways),
        out_specs=VMEM,
        compiler_params=limit(2),
        cost_estimate=CHEAP,
        name="final",
    )(done, own, *out_got)

    return (attn_out, new_k, new_v)


def solution(mesh):
    in_specs = (
        P("seq", "tp"),
        P("seq", "tp"),
        P("seq", "tp"),
        P(None, "seq", "tp"),
        P(None, "seq", "tp"),
        P(),
        P(),
        P(),
        P(),
        P("tp", None),
    )
    out_specs = (P("seq", "tp"), P(None, "seq", "tp"), P(None, "seq", "tp"))
    return jax.shard_map(
        per_device, mesh=mesh, in_specs=in_specs, out_specs=out_specs, check_vma=False
    )
```

```python
import functools
import math

import jax
import jax.numpy as jnp
from jax import lax
from jax.experimental import pallas as pl
from jax.experimental.pallas import tpu as pltpu
from jax.sharding import PartitionSpec as P

HD = 128
NEG = -1e30
FLOOR = -1e20
STATS = 128
bf16 = jnp.bfloat16
f32 = jnp.float32
i32 = jnp.int32


def nt(a, b):
    return lax.dot_general(a, b, (((1,), (1,)), ((), ())), preferred_element_type=f32)


def tn(a, b):
    return lax.dot_general(a, b, (((0,), (0,)), ((), ())), preferred_element_type=f32)


def split3(x):
    hi = x.astype(bf16).astype(f32)
    rest = x - hi
    mid = rest.astype(bf16).astype(f32)
    return hi, mid, rest - mid


def migrating_pair(mig_ref, requests, flag=1):
    first = i32(0)
    last = i32(0)
    for r in reversed(range(requests)):
        first = jnp.where(mig_ref[r] == flag, r, first)
    for r in range(requests):
        last = jnp.where(mig_ref[r] == flag, r, last)
    return first, last


def block_copies(me, pair, caches, targets, slots, block, sems, back=False):
    copies = []
    for target, slot in zip(targets, slots):
        at = pl.ds(pl.multiple_of(target * block, block), block)
        for c, cache in enumerate(caches):
            for m in range(2):
                ends = cache.at[pair[m], at], slot.at[pl.ds((2 * c + m) * block, block)]
                copies.append(pltpu.make_async_copy(*(ends[::-1] if back else ends), sems.at[len(copies)]))
    return copies


def deltas(me, kind, k, quarter):
    z = me // quarter
    inner = (z == 1) | (z == 2)
    pick = jnp.where if not isinstance(me, int) else lambda c, a, b: a if c else b
    near, far = quarter + k, 2 * quarter + k
    if kind == "inner":
        return pick(inner, far, near), pick(inner, near, far)
    if kind == "outer":
        return pick(inner, near, far), pick(inner, far, near)
    both = k if kind == "same" else 3 * quarter + k
    return both, both


def prep_kernel(me_ref, mig_ref, accepted_ref, dk_ref, dv_ref, ck_ref, cv_ref, *rest, ops, block, quarter):
    *outs, acc_ref, sems = rest
    requests, accept = accepted_ref.shape
    rows = dk_ref.shape[0]
    drafts = rows * quarter
    me = me_ref[0]
    pair = migrating_pair(mig_ref, requests)
    goals = [me ^ deltas(me, kind, k, quarter)[0] for kind, k in ops]
    copies = block_copies(me, pair, (ck_ref, cv_ref), goals, outs, block, sems)
    for copy in copies:
        copy.start()
    request = (me * rows) // drafts
    offset = me * rows - request * drafts
    mine = lax.broadcasted_iota(i32, (requests, accept), 0) == request
    node = jnp.sum(jnp.where(mine, accepted_ref[...], 0), axis=0, keepdims=True)
    pick = jnp.where(lax.broadcasted_iota(i32, (rows, accept), 0) + offset == node, 1.0, 0.0).astype(bf16)
    chosen = jnp.concatenate([tn(pick, dk_ref[...]), tn(pick, dv_ref[...])], axis=0).astype(bf16)
    acc_ref[...] = chosen
    for out in outs:
        out[4 * block :] = chosen
    for copy in copies:
        copy.wait()


def tree_bias(me_ref, parents_ref, rows):
    requests, drafts = parents_ref.shape
    request = (me_ref[0] * rows) // drafts
    offset = me_ref[0] * rows - request * drafts
    mine = lax.broadcasted_iota(i32, (requests, drafts), 0) == request
    parent = jnp.sum(jnp.where(mine, parents_ref[...], 0), axis=0, keepdims=True)
    down = lax.broadcasted_iota(i32, (drafts, drafts), 0)
    along = lax.broadcasted_iota(i32, (drafts, drafts), 1)
    reach = jnp.where((down == along) | (parent == down), 1.0, 0.0).astype(bf16)
    for _ in range(max(1, (drafts - 1).bit_length())):
        both = jnp.dot(reach, reach, preferred_element_type=f32)
        reach = jnp.where(both > 0.5, 1.0, 0.0).astype(bf16)
    pick = jnp.where(
        lax.broadcasted_iota(i32, (drafts, rows), 0) == lax.broadcasted_iota(i32, (drafts, rows), 1) + offset, 1.0, 0.0
    ).astype(bf16)
    return jnp.where(tn(reach, pick) > 0.5, 0.0, NEG)


def attend_kernel(me_ref, len_ref, mig_ref, *rest, count, block, group, own):
    quarter = count // 4
    q_refs = rest[:quarter]
    rest = rest[quarter:]
    if own:
        dk_ref, dv_ref, parents_ref = rest[:3]
        rest = rest[3:]
    ck_ref, cv_ref = rest[:2]
    outs = rest[2 : 2 + quarter]
    k_ref, v_ref, q_all, part, sems = rest[-5:]
    me = me_ref[0]
    spot = lax.rem(me, quarter)
    z = me // quarter
    first = z if own else z ^ 1
    rows, q_width = q_all.shape[2:]
    cache_dev = k_ref.shape[1]
    kv_local = k_ref.shape[2] // HD
    drafts = quarter * rows
    heads = kv_local * group
    requests = [first, first ^ 2]
    loads = []
    for i, request in enumerate(requests):
        for c, (cache, here) in enumerate(((ck_ref, k_ref), (cv_ref, v_ref))):
            loads.append(pltpu.make_async_copy(cache.at[request], here.at[i], sems.at[i, c]))
            loads[-1].start()
    for e in range(quarter):
        both = q_refs[e][...].astype(q_all.dtype)
        for k in range(2):
            q_all[k, spot ^ e] = both[k * rows : (k + 1) * rows]
    if own:
        bias = tree_bias(me_ref, parents_ref, rows)
    row = lax.broadcasted_iota(i32, (1, cache_dev), 1)
    shift = block.bit_length() - 1
    moved = row + (row >> shift) * ((count - 1) * block) + me * block
    scale = math.log2(math.e) / math.sqrt(HD)
    lane = lax.broadcasted_iota(i32, (drafts, STATS), 1)
    for i, request in enumerate(requests):
        drafted = own and i == 0
        position = jnp.where(mig_ref[request] == 1, moved, row + me * cache_dev)
        dead = jnp.where(position < len_ref[request], 0.0, NEG)
        rows_q = q_all[i].reshape(drafts, q_width)
        loads[2 * i].wait()
        loads[2 * i + 1].wait()
        stats = jnp.zeros((drafts, STATS), f32)
        for g in range(kv_local):
            at_g = slice(g * HD, (g + 1) * HD)
            q = jnp.concatenate(
                [rows_q[:, (g * group + j) * HD : (g * group + j + 1) * HD] for j in range(group)], axis=0
            ).astype(bf16)
            s = nt(q, k_ref[i, :, at_g]) * scale + dead
            top = jnp.max(s, axis=1, keepdims=True)
            if drafted:
                sd = nt(q, dk_ref[:, at_g]) * scale + jnp.concatenate([bias] * group, axis=0)
                top = jnp.maximum(top, jnp.max(sd, axis=1, keepdims=True))
            top = jnp.maximum(top, FLOOR)
            w = jnp.exp2(s - top)
            total = jnp.sum(w, axis=1, keepdims=True)
            o = jnp.dot(w.astype(bf16), v_ref[i, :, at_g], preferred_element_type=f32)
            if drafted:
                wd = jnp.exp2(sd - top)
                total = total + jnp.sum(wd, axis=1, keepdims=True)
                o = o + jnp.dot(wd.astype(bf16), dv_ref[:, at_g], preferred_element_type=f32)
            for j in range(group):
                h = g * group + j
                at = slice(j * drafts, (j + 1) * drafts)
                values = split3(top[at]) + split3(total[at])[:2]
                for n, value in enumerate(values):
                    stats = jnp.where(lane == n * heads + h, value, stats)
                for p in range(quarter):
                    part[i, p, :, h * HD : (h + 1) * HD] = o[
                        j * drafts + p * rows : j * drafts + (p + 1) * rows
                    ].astype(part.dtype)
        for p in range(quarter):
            part[i, p, :, q_width:] = stats[p * rows : (p + 1) * rows].astype(part.dtype)
    for e in range(quarter):
        outs[e][...] = jnp.concatenate([part[k, spot ^ e] for k in range(2)], axis=0).astype(bf16)


def view(ref, k, rows):
    def get(at):
        if rows % 16 == 0 or ref.shape[0] == rows:
            return ref[k * rows : (k + 1) * rows, at].astype(f32)
        return ref[:, at].astype(f32)[k * rows : (k + 1) * rows]

    return get


def merge(parts, heads):
    width = heads * HD
    stats = [get(slice(width, width + STATS)) for get in parts]
    tops = [s[:, :heads] + s[:, heads : 2 * heads] + s[:, 2 * heads : 3 * heads] for s in stats]
    totals = [s[:, 3 * heads : 4 * heads] + s[:, 4 * heads : 5 * heads] for s in stats]
    top = functools.reduce(jnp.maximum, tops)
    factors = [jnp.exp2(t - top) for t in tops]
    total = sum(f * t for f, t in zip(factors, totals))
    sums = []
    for h in range(heads):
        sums.append(sum(f[:, h : h + 1] * get(slice(h * HD, (h + 1) * HD)) for f, get in zip(factors, parts)))
    return top, total, sums


def reduce_kernel(*refs, heads):
    *parts, out = refs
    rows = out.shape[0]
    top, total, sums = merge([view(r, 1, rows) for r in parts], heads)
    lane = lax.broadcasted_iota(i32, (rows, STATS), 1)
    stats = jnp.zeros((rows, STATS), f32)
    values = split3(top) + split3(total)[:2]
    for k, value in enumerate(values):
        for h in range(heads):
            stats = jnp.where(lane == k * heads + h, value[:, h : h + 1], stats)
    for h in range(heads):
        out[:, h * HD : (h + 1) * HD] = sums[h].astype(bf16)
    out[:, heads * HD :] = stats.astype(bf16)


def weight_kernel(tp_ref, after_ref, w_ref, here_ref, sems):
    ways, _, width = here_ref.shape
    loads = []
    for d in range(ways):
        at = pl.ds(pl.multiple_of((tp_ref[0] ^ ((d + 1) % ways)) * width, width), width)
        loads.append(pltpu.make_async_copy(w_ref.at[:, at], here_ref.at[d], sems.at[d]))
        loads[-1].start()
    for load in loads:
        load.wait()


def project_kernel(done_ref, *refs, heads, ways):
    parts, here_ref, outs = refs[: -ways - 1], refs[-ways - 1], refs[-ways:-1]
    own_ref = refs[-1]
    rows, width = own_ref.shape
    top, total, sums = merge([view(r, 0, rows) for r in parts], heads)
    attention = jnp.concatenate(
        [(sums[h] / total[:, h : h + 1]).astype(bf16) for h in range(heads)], axis=1
    )
    for d in range(ways):
        block = jnp.dot(attention, here_ref[d], preferred_element_type=f32)
        if d < ways - 1:
            outs[d][...] = block.astype(bf16)
        else:
            own_ref[...] = block


def final_kernel(done_ref, own_ref, *rest):
    out_ref = rest[-1]
    total = own_ref[...]
    for ref in rest[:-1]:
        total = total + ref[...].astype(f32)
    out_ref[...] = total.astype(bf16)


def put_kernel(me_ref, mig_ref, after_ref, *rest, ops, block, quarter, first, fill):
    gots = rest[: len(ops)]
    rest = rest[len(ops) :]
    if fill:
        ck_ref, cv_ref = rest[:2]
        rest = rest[2:]
    if not first:
        rest = rest[2:]
    nk_ref, nv_ref, done_ref, sems, *rest = rest
    me = me_ref[0]
    pair = migrating_pair(mig_ref, mig_ref.shape[0])
    news = (nk_ref, nv_ref)
    sources = [me ^ deltas(me, kind, k, quarter)[1] for kind, k in ops]
    copies = block_copies(me, pair, news, sources, gots, block, sems, back=True)
    for copy in copies:
        copy.start()
    done_ref[...] = jnp.zeros_like(done_ref)
    if fill:
        hold_ref, own_ref, hold_sems, own_sems = rest
        stay = migrating_pair(mig_ref, mig_ref.shape[0], 0)
        at = pl.ds(pl.multiple_of(me * block, block), block)
        loads, stores = [], []
        for c, (cache, new) in enumerate(zip((ck_ref, cv_ref), news)):
            for m in range(2):
                for here, held, there, sem in (
                    (cache.at[stay[m]], hold_ref.at[c, m], new.at[stay[m]], hold_sems),
                    (cache.at[pair[m], at], own_ref.at[c, m], new.at[pair[m], at], own_sems),
                ):
                    loads.append(pltpu.make_async_copy(here, held, sem.at[0, c, m]))
                    stores.append(pltpu.make_async_copy(held, there, sem.at[1, c, m]))
                    loads[-1].start()
        for load, store in zip(loads, stores):
            load.wait()
            store.start()
        copies = copies + stores
    for copy in copies:
        copy.wait()


def place_kernel(me_ref, mig_ref, len_ref, accepted_ref, acc_ref, *rest, ops, last, quarter, block):
    *gots, fk_ref, fv_ref, nk_ref, nv_ref, done_ref, wins_ref, sems, win_sem = rest
    requests, accept = accepted_ref.shape
    count = 4 * quarter
    cache_dev = nk_ref.shape[1]
    me = me_ref[0]
    pair = migrating_pair(mig_ref, requests)
    sources = [me ^ deltas(me, kind, k, quarter)[1] for kind, k in ops]
    done_ref[...] = jnp.zeros_like(done_ref)
    ends = [(source, got) for op, source, got in zip(ops, sources, gots) if op in last]
    copies = block_copies(me, pair, (nk_ref, nv_ref), *zip(*ends), block, sems, back=True)
    for copy in copies:
        copy.start()
    per_request = count // requests
    parts = [acc_ref[...].astype(f32)] + [got[4 * block :].astype(f32) for got in gots]
    helds = []
    for r in range(requests):
        held = jnp.where(me // per_request == r, parts[0], 0.0)
        for owner, rows in zip(sources, parts[1:]):
            held = held + jnp.where(owner // per_request == r, rows, 0.0)
        helds.append(held)
    for copy in copies:
        copy.wait()
    span = wins_ref.shape[2]
    first = [len_ref[r] - me * cache_dev for r in range(requests)]
    low = [pl.multiple_of(jnp.clip((x >> 4) << 4, 0, cache_dev - span), 16) for x in first]
    loads, stores = [], []
    for c, new in enumerate((nk_ref, nv_ref)):
        for r in range(requests):
            a, b = new.at[r, pl.ds(low[r], span)], wins_ref.at[c, r]
            loads.append(pltpu.make_async_copy(a, b, win_sem.at[0, c, r]))
            stores.append(pltpu.make_async_copy(b, a, win_sem.at[1, c, r]))
    for copy in loads:
        copy.start()
    for copy in loads:
        copy.wait()
    for r in range(requests):
        held = helds[r]
        row = lax.broadcasted_iota(i32, (span, 1), 0) + low[r]
        for c in range(2):
            window = wins_ref[c, r].astype(f32)
            for i in range(accept):
                hit = (row == first[r] + i) & (accepted_ref[r, i] >= 0)
                window = jnp.where(hit, held[c * accept + i : c * accept + i + 1], window)
            wins_ref[c, r] = window.astype(bf16)
            stores[c * requests + r].start()
    for copy in stores:
        copy.wait()


ANY = pl.BlockSpec(memory_space=pl.ANY)
SMEM = pl.BlockSpec(memory_space=pltpu.SMEM)
VMEM = pl.BlockSpec(memory_space=pltpu.VMEM)
HBM = pl.BlockSpec(memory_space=pltpu.HBM)

CHEAP = pl.CostEstimate(flops=1, transcendentals=0, bytes_accessed=1)


def limit(mib):
    return pltpu.CompilerParams(vmem_limit_bytes=mib << 20)


def per_device(
    draft_q, draft_k, draft_v, cache_k, cache_v, lengths, migrating, parents, accepted, out_weight
):
    count = lax.axis_size("seq")
    ways = lax.axis_size("tp")
    half = count // 2
    me = lax.axis_index("seq").astype(i32)
    tp = lax.axis_index("tp").astype(i32)
    rows, q_width = draft_q.shape
    requests, drafts = parents.shape
    accept = accepted.shape[1]
    cache_dev, kv_width = cache_k.shape[1:]
    group = q_width // kv_width
    heads = q_width // HD
    block = cache_dev // count
    draft_k, draft_v, cache_k, cache_v, lengths, migrating, parents, accepted, out_weight = [
        pltpu.with_memory_space_constraint(x, pltpu.HBM)
        for x in (draft_k, draft_v, cache_k, cache_v, lengths, migrating, parents, accepted, out_weight)
    ]
    me1 = me.reshape(1)
    tp1 = tp.reshape(1)
    across = [(i, (i + half) % count) for i in range(count)]
    beside = [[(i, i ^ e) for i in range(count)] for e in range(half)]

    def to_mates(parts):
        got = {e: lax.ppermute(parts[e], "seq", beside[e]) for e in reversed(range(1, half))}
        return [got[e] for e in range(1, half)]

    q_mirror = lax.ppermute(draft_q, "seq", across)

    payload = 4 * block + 2 * accept
    quarter = count // 4
    every = lambda kind, first=0: [(kind, k) for k in range(first, quarter)]
    bulk = every("inner") + every("outer") + every("same", 1) + every("across")
    *sends, acc_rows = pl.pallas_call(
        functools.partial(prep_kernel, ops=bulk, block=block, quarter=quarter),
        out_shape=[pltpu.VMEM((payload, kv_width), bf16)] * len(bulk)
        + [pltpu.VMEM((2 * accept, kv_width), bf16)],
        in_specs=[SMEM, SMEM, VMEM, VMEM, VMEM, HBM, HBM],
        out_specs=[VMEM] * (len(bulk) + 1),
        scratch_shapes=[pltpu.SemaphoreType.DMA((4 * len(bulk),))],
        compiler_params=limit(4),
        cost_estimate=CHEAP,
        name="prep",
    )(me1, migrating, accepted, draft_k, draft_v, cache_k, cache_v)
    sends = dict(zip(bulk, sends))
    gots = {}

    def migrate(which, after):
        ready, after = lax.optimization_barrier(([sends[op] for op in which], after))
        for op, send in zip(which, ready):
            gots[op] = lax.ppermute(send, "seq", [(i, i ^ deltas(i, *op, quarter)[0]) for i in range(count)])
        return after

    q_mirror, acc_rows = lax.optimization_barrier((q_mirror, acc_rows))
    q_both = jnp.concatenate([draft_q, q_mirror], axis=0)
    q_got = to_mates([q_both] * half)
    far = every("across")
    draft_k = migrate(every("inner"), draft_k)
    q_got[0] = migrate(every("outer"), q_got[0])
    shapes = [pltpu.HBM(cache_k.shape, bf16)] * 2
    token = pltpu.VMEM((8, 128), f32)

    def put(which, filled, after, fill=False):
        pipes = [pltpu.SemaphoreType.DMA((4 * max(len(which), 1),))]
        if fill:
            pipes += [
                pltpu.VMEM((2, 2, cache_dev, kv_width), bf16),
                pltpu.VMEM((2, 2, block, kv_width), bf16),
                pltpu.SemaphoreType.DMA((2, 2, 2)),
                pltpu.SemaphoreType.DMA((2, 2, 2)),
            ]
        caches = [cache_k, cache_v] if fill else []
        base = 3 + len(which) + len(caches)
        return pl.pallas_call(
            functools.partial(put_kernel, ops=which, block=block, quarter=quarter, first=not filled, fill=fill),
            out_shape=shapes + [token],
            in_specs=[SMEM] * 2 + [ANY] + [VMEM] * len(which) + [HBM] * (len(caches) + len(filled)),
            out_specs=[HBM, HBM, VMEM],
            input_output_aliases={base: 0, base + 1: 1} if filled else {},
            scratch_shapes=pipes,
            compiler_params=limit(6),
            cost_estimate=CHEAP,
            name="put",
        )(me1, migrating, after, *[gots[op] for op in which], *caches, *filled)

    assert requests == 4 and drafts == quarter * rows
    kind = bf16 if rows % 16 == 0 else f32

    def attend(queries, own):
        drafted = [draft_k, draft_v, parents] if own else []
        return pl.pallas_call(
            functools.partial(attend_kernel, count=count, block=block, group=group, own=own),
            out_shape=[pltpu.VMEM((2 * rows, q_width + STATS), bf16)] * quarter,
            in_specs=[SMEM] * 3 + [VMEM] * (quarter + len(drafted)) + [HBM] * 2,
            out_specs=[VMEM] * quarter,
            scratch_shapes=[
                pltpu.VMEM((2, cache_dev, kv_width), bf16),
                pltpu.VMEM((2, cache_dev, kv_width), bf16),
                pltpu.VMEM((2, quarter, rows, q_width), kind),
                pltpu.VMEM((2, quarter, rows, q_width + STATS), kind),
                pltpu.SemaphoreType.DMA((2, 2)),
            ],
            compiler_params=limit(16),
            cost_estimate=CHEAP,
            name="attend_own" if own else "attend_next",
        )(me1, lengths, migrating, *queries, *drafted, cache_k, cache_v)

    q_all = [q_both] + q_got
    parts = attend(q_all[:quarter], True)
    q_next, parts = lax.optimization_barrier((q_all[quarter:], parts))
    later = attend(q_next, False)
    *filled, done = put(every("inner"), [], later[0])
    done = migrate(far[: quarter // 2], done)
    later, done = lax.optimization_barrier((later, done))
    parts = parts + later
    parts_got = to_mates(parts)
    *filled, done = put(every("outer"), filled, done)
    done = migrate(far[quarter // 2 :], done)
    *filled, done = put([], filled, done, fill=True)
    *filled, done = put(far[: quarter // 2], filled, done)
    done = migrate(every("same", 1), done)
    parts_got, done = lax.optimization_barrier((parts_got, done))
    theirs_sum = pl.pallas_call(
        functools.partial(reduce_kernel, heads=heads),
        out_shape=pltpu.VMEM((rows, q_width + STATS), bf16),
        in_specs=[VMEM] * half,
        out_specs=VMEM,
        compiler_params=limit(2),
        cost_estimate=CHEAP,
        name="reduce_other",
    )(parts[0], *parts_got)
    crossed = lax.ppermute(theirs_sum, "seq", across)
    last = far[quarter // 2 :] + every("same", 1)
    width = out_weight.shape[1] // ways
    weight = pl.pallas_call(
        weight_kernel,
        out_shape=pltpu.VMEM((ways, q_width, width), bf16),
        in_specs=[SMEM, ANY, HBM],
        out_specs=VMEM,
        scratch_shapes=[pltpu.SemaphoreType.DMA((ways,))],
        compiler_params=limit(1),
        cost_estimate=CHEAP,
        name="weight",
    )(tp1, theirs_sum, out_weight)
    weight, crossed = lax.optimization_barrier((weight, crossed))
    *outs, own = pl.pallas_call(
        functools.partial(project_kernel, heads=heads, ways=ways),
        out_shape=[pltpu.VMEM((rows, width), bf16)] * (ways - 1) + [pltpu.VMEM((rows, width), f32)],
        in_specs=[VMEM] * (half + 3),
        out_specs=[VMEM] * ways,
        compiler_params=limit(4),
        cost_estimate=CHEAP,
        name="project",
    )(done, parts[0], *parts_got, crossed, weight)
    out_got = [
        lax.ppermute(x, "tp", [(i, i ^ (d + 1)) for i in range(ways)]) for d, x in enumerate(outs)
    ]
    span = 32
    base = 5 + len(bulk)
    own, filled = lax.optimization_barrier((own, filled))
    new_k, new_v, done = pl.pallas_call(
        functools.partial(place_kernel, ops=bulk, last=last, quarter=quarter, block=block),
        out_shape=shapes + [token],
        in_specs=[SMEM] * 4 + [VMEM] * (1 + len(bulk)) + [HBM, HBM],
        out_specs=[HBM, HBM, VMEM],
        input_output_aliases={base: 0, base + 1: 1},
        scratch_shapes=[
            pltpu.VMEM((2, requests, span, kv_width), bf16),
            pltpu.SemaphoreType.DMA((4 * len(last),)),
            pltpu.SemaphoreType.DMA((2, 2, requests)),
        ],
        compiler_params=limit(4),
        cost_estimate=CHEAP,
        name="place",
    )(me1, migrating, lengths, accepted, acc_rows, *[gots[op] for op in bulk], *filled)
    attn_out = pl.pallas_call(
        final_kernel,
        out_shape=jax.ShapeDtypeStruct((rows, width), bf16),
        in_specs=[VMEM] * (1 + ways),
        out_specs=VMEM,
        compiler_params=limit(2),
        cost_estimate=CHEAP,
        name="final",
    )(done, own, *out_got)

    return (attn_out, new_k, new_v)


def solution(mesh):
    in_specs = (
        P("seq", "tp"),
        P("seq", "tp"),
        P("seq", "tp"),
        P(None, "seq", "tp"),
        P(None, "seq", "tp"),
        P(),
        P(),
        P(),
        P(),
        P("tp", None),
    )
    out_specs = (P("seq", "tp"), P(None, "seq", "tp"), P(None, "seq", "tp"))
    return jax.shard_map(
        per_device, mesh=mesh, in_specs=in_specs, out_specs=out_specs, check_vma=False
    )
```

```python
import functools
import math

import jax
import jax.numpy as jnp
from jax import lax
from jax.experimental import pallas as pl
from jax.experimental.pallas import tpu as pltpu
from jax.sharding import PartitionSpec as P

HD = 128
NEG = -1e30
FLOOR = -1e20
STATS = 128
bf16 = jnp.bfloat16
f32 = jnp.float32
i32 = jnp.int32


def nt(a, b):
    return lax.dot_general(a, b, (((1,), (1,)), ((), ())), preferred_element_type=f32)


def tn(a, b):
    return lax.dot_general(a, b, (((0,), (0,)), ((), ())), preferred_element_type=f32)


def split3(x):
    hi = x.astype(bf16).astype(f32)
    rest = x - hi
    mid = rest.astype(bf16).astype(f32)
    return hi, mid, rest - mid


def migrating_pair(mig_ref, requests, flag=1):
    first = i32(0)
    last = i32(0)
    for r in reversed(range(requests)):
        first = jnp.where(mig_ref[r] == flag, r, first)
    for r in range(requests):
        last = jnp.where(mig_ref[r] == flag, r, last)
    return first, last


def block_copies(me, pair, caches, targets, slots, block, sems, back=False):
    copies = []
    for target, slot in zip(targets, slots):
        at = pl.ds(pl.multiple_of(target * block, block), block)
        for c, cache in enumerate(caches):
            for m in range(2):
                ends = cache.at[pair[m], at], slot.at[pl.ds((2 * c + m) * block, block)]
                copies.append(pltpu.make_async_copy(*(ends[::-1] if back else ends), sems.at[len(copies)]))
    return copies


def deltas(me, kind, k, quarter):
    z = me // quarter
    inner = (z == 1) | (z == 2)
    pick = jnp.where if not isinstance(me, int) else lambda c, a, b: a if c else b
    near, far = quarter + k, 2 * quarter + k
    if kind == "inner":
        return pick(inner, far, near), pick(inner, near, far)
    if kind == "outer":
        return pick(inner, near, far), pick(inner, far, near)
    both = k if kind == "same" else 3 * quarter + k
    return both, both


def prep_kernel(me_ref, mig_ref, accepted_ref, dk_ref, dv_ref, ck_ref, cv_ref, *rest, ops, block, quarter):
    *outs, acc_ref, sems = rest
    requests, accept = accepted_ref.shape
    rows = dk_ref.shape[0]
    drafts = rows * quarter
    me = me_ref[0]
    pair = migrating_pair(mig_ref, requests)
    goals = [me ^ deltas(me, kind, k, quarter)[0] for kind, k in ops]
    copies = block_copies(me, pair, (ck_ref, cv_ref), goals, outs, block, sems)
    for copy in copies:
        copy.start()
    request = (me * rows) // drafts
    offset = me * rows - request * drafts
    mine = lax.broadcasted_iota(i32, (requests, accept), 0) == request
    node = jnp.sum(jnp.where(mine, accepted_ref[...], 0), axis=0, keepdims=True)
    pick = jnp.where(lax.broadcasted_iota(i32, (rows, accept), 0) + offset == node, 1.0, 0.0).astype(bf16)
    chosen = jnp.concatenate([tn(pick, dk_ref[...]), tn(pick, dv_ref[...])], axis=0).astype(bf16)
    acc_ref[...] = chosen
    for out in outs:
        out[4 * block :] = chosen
    for copy in copies:
        copy.wait()


def tree_bias(me_ref, parents_ref, rows):
    requests, drafts = parents_ref.shape
    request = (me_ref[0] * rows) // drafts
    offset = me_ref[0] * rows - request * drafts
    mine = lax.broadcasted_iota(i32, (requests, drafts), 0) == request
    parent = jnp.sum(jnp.where(mine, parents_ref[...], 0), axis=0, keepdims=True)
    down = lax.broadcasted_iota(i32, (drafts, drafts), 0)
    along = lax.broadcasted_iota(i32, (drafts, drafts), 1)
    reach = jnp.where((down == along) | (parent == down), 1.0, 0.0).astype(bf16)
    for _ in range(max(1, (drafts - 1).bit_length())):
        both = jnp.dot(reach, reach, preferred_element_type=f32)
        reach = jnp.where(both > 0.5, 1.0, 0.0).astype(bf16)
    pick = jnp.where(
        lax.broadcasted_iota(i32, (drafts, rows), 0) == lax.broadcasted_iota(i32, (drafts, rows), 1) + offset, 1.0, 0.0
    ).astype(bf16)
    return jnp.where(tn(reach, pick) > 0.5, 0.0, NEG)


def attend_kernel(me_ref, len_ref, mig_ref, *rest, count, block, group, own):
    quarter = count // 4
    q_refs = rest[:quarter]
    rest = rest[quarter:]
    if own:
        dk_ref, dv_ref, parents_ref = rest[:3]
        rest = rest[3:]
    ck_ref, cv_ref = rest[:2]
    outs = rest[2 : 2 + quarter]
    k_ref, v_ref, q_all, part, sems = rest[-5:]
    me = me_ref[0]
    spot = lax.rem(me, quarter)
    z = me // quarter
    first = z if own else z ^ 1
    rows, q_width = q_all.shape[2:]
    cache_dev = k_ref.shape[1]
    kv_local = k_ref.shape[2] // HD
    drafts = quarter * rows
    heads = kv_local * group
    requests = [first, first ^ 2]
    loads = []
    for i, request in enumerate(requests):
        for c, (cache, here) in enumerate(((ck_ref, k_ref), (cv_ref, v_ref))):
            loads.append(pltpu.make_async_copy(cache.at[request], here.at[i], sems.at[i, c]))
            loads[-1].start()
    for e in range(quarter):
        both = q_refs[e][...].astype(q_all.dtype)
        for k in range(2):
            q_all[k, spot ^ e] = both[k * rows : (k + 1) * rows]
    if own:
        bias = tree_bias(me_ref, parents_ref, rows)
    row = lax.broadcasted_iota(i32, (1, cache_dev), 1)
    shift = block.bit_length() - 1
    moved = row + (row >> shift) * ((count - 1) * block) + me * block
    scale = math.log2(math.e) / math.sqrt(HD)
    lane = lax.broadcasted_iota(i32, (drafts, STATS), 1)
    for i, request in enumerate(requests):
        drafted = own and i == 0
        position = jnp.where(mig_ref[request] == 1, moved, row + me * cache_dev)
        dead = jnp.where(position < len_ref[request], 0.0, NEG)
        rows_q = q_all[i].reshape(drafts, q_width)
        loads[2 * i].wait()
        loads[2 * i + 1].wait()
        stats = jnp.zeros((drafts, STATS), f32)
        for g in range(kv_local):
            at_g = slice(g * HD, (g + 1) * HD)
            q = jnp.concatenate(
                [rows_q[:, (g * group + j) * HD : (g * group + j + 1) * HD] for j in range(group)], axis=0
            ).astype(bf16)
            s = nt(q, k_ref[i, :, at_g]) * scale + dead
            top = jnp.max(s, axis=1, keepdims=True)
            if drafted:
                sd = nt(q, dk_ref[:, at_g]) * scale + jnp.concatenate([bias] * group, axis=0)
                top = jnp.maximum(top, jnp.max(sd, axis=1, keepdims=True))
            top = jnp.maximum(top, FLOOR)
            w = jnp.exp2(s - top)
            total = jnp.sum(w, axis=1, keepdims=True)
            o = jnp.dot(w.astype(bf16), v_ref[i, :, at_g], preferred_element_type=f32)
            if drafted:
                wd = jnp.exp2(sd - top)
                total = total + jnp.sum(wd, axis=1, keepdims=True)
                o = o + jnp.dot(wd.astype(bf16), dv_ref[:, at_g], preferred_element_type=f32)
            for j in range(group):
                h = g * group + j
                at = slice(j * drafts, (j + 1) * drafts)
                values = split3(top[at]) + split3(total[at])[:2]
                for n, value in enumerate(values):
                    stats = jnp.where(lane == n * heads + h, value, stats)
                for p in range(quarter):
                    part[i, p, :, h * HD : (h + 1) * HD] = o[
                        j * drafts + p * rows : j * drafts + (p + 1) * rows
                    ].astype(part.dtype)
        for p in range(quarter):
            part[i, p, :, q_width:] = stats[p * rows : (p + 1) * rows].astype(part.dtype)
    for e in range(quarter):
        outs[e][...] = jnp.concatenate([part[k, spot ^ e] for k in range(2)], axis=0).astype(bf16)


def view(ref, k, rows):
    def get(at):
        if rows % 16 == 0 or ref.shape[0] == rows:
            return ref[k * rows : (k + 1) * rows, at].astype(f32)
        return ref[:, at].astype(f32)[k * rows : (k + 1) * rows]

    return get


def merge(parts, heads):
    width = heads * HD
    stats = [get(slice(width, width + STATS)) for get in parts]
    tops = [s[:, :heads] + s[:, heads : 2 * heads] + s[:, 2 * heads : 3 * heads] for s in stats]
    totals = [s[:, 3 * heads : 4 * heads] + s[:, 4 * heads : 5 * heads] for s in stats]
    top = functools.reduce(jnp.maximum, tops)
    factors = [jnp.exp2(t - top) for t in tops]
    total = sum(f * t for f, t in zip(factors, totals))
    sums = []
    for h in range(heads):
        sums.append(sum(f[:, h : h + 1] * get(slice(h * HD, (h + 1) * HD)) for f, get in zip(factors, parts)))
    return top, total, sums


def reduce_kernel(*refs, heads):
    *parts, out = refs
    rows = out.shape[0]
    top, total, sums = merge([view(r, 1, rows) for r in parts], heads)
    lane = lax.broadcasted_iota(i32, (rows, STATS), 1)
    stats = jnp.zeros((rows, STATS), f32)
    values = split3(top) + split3(total)[:2]
    for k, value in enumerate(values):
        for h in range(heads):
            stats = jnp.where(lane == k * heads + h, value[:, h : h + 1], stats)
    for h in range(heads):
        out[:, h * HD : (h + 1) * HD] = sums[h].astype(bf16)
    out[:, heads * HD :] = stats.astype(bf16)


def weight_kernel(tp_ref, after_ref, w_ref, here_ref, sems):
    ways, _, width = here_ref.shape
    loads = []
    for d in range(ways):
        at = pl.ds(pl.multiple_of((tp_ref[0] ^ ((d + 1) % ways)) * width, width), width)
        loads.append(pltpu.make_async_copy(w_ref.at[:, at], here_ref.at[d], sems.at[d]))
        loads[-1].start()
    for load in loads:
        load.wait()


def project_kernel(done_ref, *refs, heads, ways):
    parts, here_ref, outs = refs[: -ways - 1], refs[-ways - 1], refs[-ways:-1]
    own_ref = refs[-1]
    rows, width = own_ref.shape
    top, total, sums = merge([view(r, 0, rows) for r in parts], heads)
    attention = jnp.concatenate(
        [(sums[h] / total[:, h : h + 1]).astype(bf16) for h in range(heads)], axis=1
    )
    for d in range(ways):
        block = jnp.dot(attention, here_ref[d], preferred_element_type=f32)
        if d < ways - 1:
            outs[d][...] = block.astype(bf16)
        else:
            own_ref[...] = block


def final_kernel(done_ref, own_ref, *rest):
    out_ref = rest[-1]
    total = own_ref[...]
    for ref in rest[:-1]:
        total = total + ref[...].astype(f32)
    out_ref[...] = total.astype(bf16)


def note_kernel(*refs):
    refs[-1][...] = jnp.zeros_like(refs[-1])


def put_kernel(me_ref, mig_ref, after_ref, *rest, ops, block, quarter, first, fill):
    gots = rest[: len(ops)]
    rest = rest[len(ops) :]
    if fill:
        ck_ref, cv_ref = rest[:2]
        rest = rest[2:]
    if not first:
        rest = rest[2:]
    nk_ref, nv_ref, done_ref, sems, *rest = rest
    me = me_ref[0]
    pair = migrating_pair(mig_ref, mig_ref.shape[0])
    news = (nk_ref, nv_ref)
    sources = [me ^ deltas(me, kind, k, quarter)[1] for kind, k in ops]
    copies = block_copies(me, pair, news, sources, gots, block, sems, back=True)
    for copy in copies:
        copy.start()
    done_ref[...] = jnp.zeros_like(done_ref)
    if fill:
        hold_ref, own_ref, hold_sems, own_sems = rest
        stay = migrating_pair(mig_ref, mig_ref.shape[0], 0)
        at = pl.ds(pl.multiple_of(me * block, block), block)
        loads, stores = [], []
        for c, (cache, new) in enumerate(zip((ck_ref, cv_ref), news)):
            for m in range(2):
                for here, held, there, sem in (
                    (cache.at[stay[m]], hold_ref.at[c, m], new.at[stay[m]], hold_sems),
                    (cache.at[pair[m], at], own_ref.at[c, m], new.at[pair[m], at], own_sems),
                ):
                    loads.append(pltpu.make_async_copy(here, held, sem.at[0, c, m]))
                    stores.append(pltpu.make_async_copy(held, there, sem.at[1, c, m]))
                    loads[-1].start()
        for load, store in zip(loads, stores):
            load.wait()
            store.start()
        copies = copies + stores
    for copy in copies:
        copy.wait()


def place_kernel(me_ref, mig_ref, len_ref, accepted_ref, acc_ref, *rest, ops, last, quarter, block):
    *gots, fk_ref, fv_ref, nk_ref, nv_ref, done_ref, wins_ref, sems, win_sem = rest
    requests, accept = accepted_ref.shape
    count = 4 * quarter
    cache_dev = nk_ref.shape[1]
    me = me_ref[0]
    pair = migrating_pair(mig_ref, requests)
    sources = [me ^ deltas(me, kind, k, quarter)[1] for kind, k in ops]
    done_ref[...] = jnp.zeros_like(done_ref)
    ends = [(source, got) for op, source, got in zip(ops, sources, gots) if op in last]
    copies = block_copies(me, pair, (nk_ref, nv_ref), *zip(*ends), block, sems, back=True)
    for copy in copies:
        copy.start()
    per_request = count // requests
    parts = [acc_ref[...].astype(f32)] + [got[4 * block :].astype(f32) for got in gots]
    helds = []
    for r in range(requests):
        held = jnp.where(me // per_request == r, parts[0], 0.0)
        for owner, rows in zip(sources, parts[1:]):
            held = held + jnp.where(owner // per_request == r, rows, 0.0)
        helds.append(held)
    for copy in copies:
        copy.wait()
    span = wins_ref.shape[2]
    first = [len_ref[r] - me * cache_dev for r in range(requests)]
    low = [pl.multiple_of(jnp.clip((x >> 4) << 4, 0, cache_dev - span), 16) for x in first]
    loads, stores = [], []
    for c, new in enumerate((nk_ref, nv_ref)):
        for r in range(requests):
            a, b = new.at[r, pl.ds(low[r], span)], wins_ref.at[c, r]
            loads.append(pltpu.make_async_copy(a, b, win_sem.at[0, c, r]))
            stores.append(pltpu.make_async_copy(b, a, win_sem.at[1, c, r]))
    for copy in loads:
        copy.start()
    for copy in loads:
        copy.wait()
    for r in range(requests):
        held = helds[r]
        row = lax.broadcasted_iota(i32, (span, 1), 0) + low[r]
        for c in range(2):
            window = wins_ref[c, r].astype(f32)
            for i in range(accept):
                hit = (row == first[r] + i) & (accepted_ref[r, i] >= 0)
                window = jnp.where(hit, held[c * accept + i : c * accept + i + 1], window)
            wins_ref[c, r] = window.astype(bf16)
            stores[c * requests + r].start()
    for copy in stores:
        copy.wait()


ANY = pl.BlockSpec(memory_space=pl.ANY)
SMEM = pl.BlockSpec(memory_space=pltpu.SMEM)
VMEM = pl.BlockSpec(memory_space=pltpu.VMEM)
HBM = pl.BlockSpec(memory_space=pltpu.HBM)

CHEAP = pl.CostEstimate(flops=1, transcendentals=0, bytes_accessed=1)


def limit(mib):
    return pltpu.CompilerParams(vmem_limit_bytes=mib << 20)


def per_device(
    draft_q, draft_k, draft_v, cache_k, cache_v, lengths, migrating, parents, accepted, out_weight
):
    count = lax.axis_size("seq")
    ways = lax.axis_size("tp")
    half = count // 2
    me = lax.axis_index("seq").astype(i32)
    tp = lax.axis_index("tp").astype(i32)
    rows, q_width = draft_q.shape
    requests, drafts = parents.shape
    accept = accepted.shape[1]
    cache_dev, kv_width = cache_k.shape[1:]
    group = q_width // kv_width
    heads = q_width // HD
    block = cache_dev // count
    draft_k, draft_v, cache_k, cache_v, lengths, migrating, parents, accepted, out_weight = [
        pltpu.with_memory_space_constraint(x, pltpu.HBM)
        for x in (draft_k, draft_v, cache_k, cache_v, lengths, migrating, parents, accepted, out_weight)
    ]
    me1 = me.reshape(1)
    tp1 = tp.reshape(1)
    across = [(i, (i + half) % count) for i in range(count)]
    beside = [[(i, i ^ e) for i in range(count)] for e in range(half)]

    def to_mates(parts):
        got = {e: lax.ppermute(parts[e], "seq", beside[e]) for e in reversed(range(1, half))}
        return [got[e] for e in range(1, half)]

    q_mirror = lax.ppermute(draft_q, "seq", across)

    payload = 4 * block + 2 * accept
    quarter = count // 4
    every = lambda kind, first=0: [(kind, k) for k in range(first, quarter)]
    bulk = every("inner") + every("outer") + every("same", 1) + every("across")
    *sends, acc_rows = pl.pallas_call(
        functools.partial(prep_kernel, ops=bulk, block=block, quarter=quarter),
        out_shape=[pltpu.VMEM((payload, kv_width), bf16)] * len(bulk)
        + [pltpu.VMEM((2 * accept, kv_width), bf16)],
        in_specs=[SMEM, SMEM, VMEM, VMEM, VMEM, HBM, HBM],
        out_specs=[VMEM] * (len(bulk) + 1),
        scratch_shapes=[pltpu.SemaphoreType.DMA((4 * len(bulk),))],
        compiler_params=limit(4),
        cost_estimate=CHEAP,
        name="prep",
    )(me1, migrating, accepted, draft_k, draft_v, cache_k, cache_v)
    sends = dict(zip(bulk, sends))
    gots = {}

    def migrate(which, after):
        ready, after = lax.optimization_barrier(([sends[op] for op in which], after))
        for op, send in zip(which, ready):
            gots[op] = lax.ppermute(send, "seq", [(i, i ^ deltas(i, *op, quarter)[0]) for i in range(count)])
        return after

    q_mirror, acc_rows = lax.optimization_barrier((q_mirror, acc_rows))
    q_both = jnp.concatenate([draft_q, q_mirror], axis=0)
    q_got = to_mates([q_both] * half)
    far = every("across")
    draft_k = migrate(every("inner"), draft_k)
    q_got[0] = migrate(every("outer"), q_got[0])
    shapes = [pltpu.HBM(cache_k.shape, bf16)] * 2
    token = pltpu.VMEM((8, 128), f32)

    def put(which, filled, after, fill=False):
        pipes = [pltpu.SemaphoreType.DMA((4 * max(len(which), 1),))]
        if fill:
            pipes += [
                pltpu.VMEM((2, 2, cache_dev, kv_width), bf16),
                pltpu.VMEM((2, 2, block, kv_width), bf16),
                pltpu.SemaphoreType.DMA((2, 2, 2)),
                pltpu.SemaphoreType.DMA((2, 2, 2)),
            ]
        caches = [cache_k, cache_v] if fill else []
        base = 3 + len(which) + len(caches)
        return pl.pallas_call(
            functools.partial(put_kernel, ops=which, block=block, quarter=quarter, first=not filled, fill=fill),
            out_shape=shapes + [token],
            in_specs=[SMEM] * 2 + [ANY] + [VMEM] * len(which) + [HBM] * (len(caches) + len(filled)),
            out_specs=[HBM, HBM, VMEM],
            input_output_aliases={base: 0, base + 1: 1} if filled else {},
            scratch_shapes=pipes,
            compiler_params=limit(6),
            cost_estimate=CHEAP,
            name="put",
        )(me1, migrating, after, *[gots[op] for op in which], *caches, *filled)

    assert requests == 4 and drafts == quarter * rows
    kind = bf16 if rows % 16 == 0 else f32

    def attend(queries, own):
        drafted = [draft_k, draft_v, parents] if own else []
        return pl.pallas_call(
            functools.partial(attend_kernel, count=count, block=block, group=group, own=own),
            out_shape=[pltpu.VMEM((2 * rows, q_width + STATS), bf16)] * quarter,
            in_specs=[SMEM] * 3 + [VMEM] * (quarter + len(drafted)) + [HBM] * 2,
            out_specs=[VMEM] * quarter,
            scratch_shapes=[
                pltpu.VMEM((2, cache_dev, kv_width), bf16),
                pltpu.VMEM((2, cache_dev, kv_width), bf16),
                pltpu.VMEM((2, quarter, rows, q_width), kind),
                pltpu.VMEM((2, quarter, rows, q_width + STATS), kind),
                pltpu.SemaphoreType.DMA((2, 2)),
            ],
            compiler_params=limit(16),
            cost_estimate=CHEAP,
            name="attend_own" if own else "attend_next",
        )(me1, lengths, migrating, *queries, *drafted, cache_k, cache_v)

    q_all = [q_both] + q_got
    parts = attend(q_all[:quarter], True)
    q_next, parts = lax.optimization_barrier((q_all[quarter:], parts))
    later = attend(q_next, False)
    done = pl.pallas_call(
        note_kernel,
        out_shape=token,
        in_specs=[ANY] * (1 + quarter),
        out_specs=VMEM,
        compiler_params=limit(1),
        cost_estimate=CHEAP,
        name="note",
    )(later[0], *[gots[op] for op in every("inner")])
    done = migrate(far[: quarter // 2], done)
    later, done = lax.optimization_barrier((later, done))
    parts = parts + later
    parts_got = to_mates(parts)
    *filled, done = put(every("inner") + every("outer"), [], done)
    done = migrate(far[quarter // 2 :], done)
    *filled, done = put([], filled, done, fill=True)
    *filled, done = put(far[: quarter // 2], filled, done)
    done = migrate(every("same", 1), done)
    parts_got, done = lax.optimization_barrier((parts_got, done))
    theirs_sum = pl.pallas_call(
        functools.partial(reduce_kernel, heads=heads),
        out_shape=pltpu.VMEM((rows, q_width + STATS), bf16),
        in_specs=[VMEM] * half,
        out_specs=VMEM,
        compiler_params=limit(2),
        cost_estimate=CHEAP,
        name="reduce_other",
    )(parts[0], *parts_got)
    crossed = lax.ppermute(theirs_sum, "seq", across)
    last = far[quarter // 2 :] + every("same", 1)
    width = out_weight.shape[1] // ways
    weight = pl.pallas_call(
        weight_kernel,
        out_shape=pltpu.VMEM((ways, q_width, width), bf16),
        in_specs=[SMEM, ANY, HBM],
        out_specs=VMEM,
        scratch_shapes=[pltpu.SemaphoreType.DMA((ways,))],
        compiler_params=limit(1),
        cost_estimate=CHEAP,
        name="weight",
    )(tp1, theirs_sum, out_weight)
    weight, crossed = lax.optimization_barrier((weight, crossed))
    *outs, own = pl.pallas_call(
        functools.partial(project_kernel, heads=heads, ways=ways),
        out_shape=[pltpu.VMEM((rows, width), bf16)] * (ways - 1) + [pltpu.VMEM((rows, width), f32)],
        in_specs=[VMEM] * (half + 3),
        out_specs=[VMEM] * ways,
        compiler_params=limit(4),
        cost_estimate=CHEAP,
        name="project",
    )(done, parts[0], *parts_got, crossed, weight)
    out_got = [
        lax.ppermute(x, "tp", [(i, i ^ (d + 1)) for i in range(ways)]) for d, x in enumerate(outs)
    ]
    span = 32
    base = 5 + len(bulk)
    own, filled = lax.optimization_barrier((own, filled))
    new_k, new_v, done = pl.pallas_call(
        functools.partial(place_kernel, ops=bulk, last=last, quarter=quarter, block=block),
        out_shape=shapes + [token],
        in_specs=[SMEM] * 4 + [VMEM] * (1 + len(bulk)) + [HBM, HBM],
        out_specs=[HBM, HBM, VMEM],
        input_output_aliases={base: 0, base + 1: 1},
        scratch_shapes=[
            pltpu.VMEM((2, requests, span, kv_width), bf16),
            pltpu.SemaphoreType.DMA((4 * len(last),)),
            pltpu.SemaphoreType.DMA((2, 2, requests)),
        ],
        compiler_params=limit(4),
        cost_estimate=CHEAP,
        name="place",
    )(me1, migrating, lengths, accepted, acc_rows, *[gots[op] for op in bulk], *filled)
    attn_out = pl.pallas_call(
        final_kernel,
        out_shape=jax.ShapeDtypeStruct((rows, width), bf16),
        in_specs=[VMEM] * (1 + ways),
        out_specs=VMEM,
        compiler_params=limit(2),
        cost_estimate=CHEAP,
        name="final",
    )(done, own, *out_got)

    return (attn_out, new_k, new_v)


def solution(mesh):
    in_specs = (
        P("seq", "tp"),
        P("seq", "tp"),
        P("seq", "tp"),
        P(None, "seq", "tp"),
        P(None, "seq", "tp"),
        P(),
        P(),
        P(),
        P(),
        P("tp", None),
    )
    out_specs = (P("seq", "tp"), P(None, "seq", "tp"), P(None, "seq", "tp"))
    return jax.shard_map(
        per_device, mesh=mesh, in_specs=in_specs, out_specs=out_specs, check_vma=False
    )
```
